128 devices in a mesh: tm: 16 (over z, x), tile: 8 (over y, core).
Axes of the slice: x: 4, y: 4, z: 4, core: 2. Of those that a mesh axis runs over, the one named last changes fastest.
Arguments:
- frames: bfloat16 [64, 64, 64, 128], P('tm', 'tile'), may hold values from -6 to 6
- cotangent: bfloat16 [64, 64, 64, 128], P('tm', 'tile'), may hold values from -6 to 6
- w_in: bfloat16 [3, 3, 128, 128], replicated, may hold values from -0.1875 to 0.1875
- w_out: bfloat16 [3, 3, 128, 128], replicated, may hold values from -0.1875 to 0.1875
- skip: float32 [128], replicated, may hold values from 0.5 to 1.5
- log_decay: float32 [64, 128], P('tm'), may hold values from -1 to 0
Outputs:
- output: bfloat16 [64, 64, 64, 128], P('tm', 'tile')
- grad_frames: bfloat16 [64, 64, 64, 128], P('tm', 'tile')
- grad_w_in: float32 [3, 3, 128, 128], replicated
- grad_w_out: float32 [3, 3, 128, 128], replicated
The draws below stay inside these ranges and needn't reach their ends.
All inputs are finite; a program needn't handle non-finite values.
Results may differ from the reference program's by a relative error of at most 0.0029.
Values may be sent and summed in bfloat16 or wider, within the bound.
A program may use at most 64 MiB of HBM per device.

```python
import math
import jax
import jax.numpy as jnp
from jax import lax

CH = 128
ST = 128
H = 64
W = 64
FRAMES = 64


def draw_log_decay(key, part):
    keys = jax.random.split(jax.random.fold_in(key, 17), 4)
    lowest = 0.1 / FRAMES
    highest = 1.0 / 25.0
    rates = jnp.exp(jax.random.uniform(keys[0], (ST,), jnp.float32, jnp.log(lowest), jnp.log(highest)))
    rough = jnp.exp(jax.random.uniform(keys[1], (FRAMES, ST), jnp.float32, jnp.log(0.5), jnp.log(2.0)))
    places = jax.random.randint(keys[2], (4,), 0, FRAMES)
    struck = jnp.any(jnp.arange(FRAMES)[:, None] == places[None, :], axis=1)
    losses = jax.random.uniform(keys[3], (FRAMES, ST), jnp.float32, jnp.log(0.5), jnp.log(0.8))
    values = -rates[None, :] * rough + jnp.where(struck[:, None], losses, 0.0)
    return values.astype(jnp.float32)


def block_scale(rng, shape, shards, low, top_value):
    level, own = 1.0, jax.random.fold_in(rng, 6)
    for position, blocks in shards:
        heights = jnp.exp(jax.random.uniform(jax.random.fold_in(own, position), (blocks,), jnp.float32, low / len(shards), top_value / len(shards)))
        level = level * jnp.repeat(heights, shape[position] // blocks).reshape([-1 if axis == position else 1 for axis in range(len(shape))])
    return level


def gaussian(stream_key, shape, spread, limit, shards=(), dtype=jnp.bfloat16):
    factor_of = block_scale(stream_key, shape, shards, -0.22, 0.18) if shards else 1.0
    array = jax.random.normal(stream_key, shape, jnp.float32) * spread * factor_of
    return jnp.minimum(jnp.maximum(array, -limit), limit).astype(dtype)


def setup_inputs(seed: int = 0) -> dict:
    arg_keys = jax.random.split(jax.random.key(seed), 7)
    frames = gaussian(arg_keys[0], (FRAMES, H, W, CH), 1.0, 6.0, ((0, 16), (1, 8)))
    cotangent = gaussian(arg_keys[1], (FRAMES, H, W, CH), 1.0, 6.0, ((0, 16), (1, 8)))
    w_in = gaussian(arg_keys[2], (3, 3, CH, ST), (9 * CH) ** -0.5, 0.1875)
    w_out = gaussian(arg_keys[3], (3, 3, ST, CH), (9 * ST) ** -0.5, 0.1875)
    skip = jnp.clip(jax.random.uniform(arg_keys[4], (CH,), jnp.float32, 0.5, 1.5), 0.5, 1.5)
    log_decay = draw_log_decay(jax.random.fold_in(arg_keys[6], 71), 0)
    return {"frames": frames, "cotangent": cotangent, "w_in": w_in, "w_out": w_out, "skip": skip, "log_decay": log_decay}


def flipped(weight):
    return jnp.transpose(weight[::-1, ::-1], (0, 1, 3, 2))

def widen(field):
    return jnp.pad(field, ((0, 0), (1, 1), (1, 1), (0, 0)))

def convolve(padded, weight):
    rows = padded.shape[1] - 2
    cols = padded.shape[2] - 2
    result = jnp.zeros((padded.shape[0], rows, cols, weight.shape[3]), jnp.float32)
    for row_off in range(3):
        for col_off in range(3):
            piece = padded[:, row_off:row_off + rows, col_off:col_off + cols, :].reshape(-1, weight.shape[2])
            result = result + jnp.dot(piece, weight[row_off, col_off], preferred_element_type=jnp.float32).reshape(result.shape)
    return result

def weight_grad(padded, target):
    rows = target.shape[1]
    cols = target.shape[2]
    flat = target.reshape(-1, target.shape[3])
    pieces = []
    for row_off in range(3):
        line = []
        for col_off in range(3):
            piece = padded[:, row_off:row_off + rows, col_off:col_off + cols, :].reshape(-1, padded.shape[3])
            line.append(lax.dot_general(piece, flat, (((0,), (0,)), ((), ())), preferred_element_type=jnp.float32))
        pieces.append(jnp.stack(line))
    return jnp.stack(pieces)

def reference(frames, cotangent, w_in, w_out, skip, log_decay):
    decay = jnp.exp(log_decay)
    frames_padded = widen(frames)
    drive = convolve(frames_padded, w_in)

    def advance(state, item):
        rate, inflow = item
        state = rate * state + (1.0 - rate) * inflow
        return (state, state)
    start = jnp.zeros(drive.shape[1:], jnp.float32)
    _, states = lax.scan(advance, start, (decay, drive))
    states_padded = widen(states.astype(jnp.bfloat16))
    output = (convolve(states_padded, w_out) + skip * frames.astype(jnp.float32)).astype(jnp.bfloat16)
    state_grad = convolve(widen(cotangent), flipped(w_out))

    def retreat(carry, item):
        rate, grad_here = item
        adjoint = grad_here + carry
        return (rate * adjoint, adjoint)
    _, adjoints = lax.scan(retreat, jnp.zeros(state_grad.shape[1:], jnp.float32), (decay, state_grad), reverse=True)
    inflow_grad = ((1.0 - decay)[:, None, None, :] * adjoints).astype(jnp.bfloat16)
    grad_frames = (convolve(widen(inflow_grad), flipped(w_in)) + skip * cotangent.astype(jnp.float32)).astype(jnp.bfloat16)
    factor = 1.0 / math.sqrt(FRAMES * H * W)
    grad_w_out = weight_grad(states_padded, cotangent) * factor
    grad_w_in = weight_grad(frames_padded, inflow_grad) * factor
    return (output, grad_frames, grad_w_in, grad_w_out)
```

```python
import functools
import math

import jax
import jax.numpy as jnp
from jax import lax
from jax.experimental import pallas as pl
from jax.experimental.pallas import tpu as pltpu
from jax.sharding import PartitionSpec as P

MESH = pl.DeviceIdType.MESH
F32 = jnp.float32
BF16 = jnp.bfloat16


def kernel(
    dims,
    frames,
    cot,
    w_in,
    w_out,
    skip,
    log_decay,
    output,
    grad_frames,
    grad_in,
    grad_out,
    F, C, S, I,
    F3, C3, S3, I3,
    WOF, WIF,
    LS, LA, OB,
    DEC, DG,
    RF, EF, INF, RB, EB, INB,
    G, R0, R1, R2, A2, R3, O2, OUT,
    OB_F, OB_C,
    load_sem, halo_send, halo_recv, carry_send, carry_recv, ar_send, ar_recv, out_sem,
):
    nt, nx, ny, factor = dims
    T, R, W, CH = frames.shape
    n = nx
    pos = R * W
    piece = pos // nt
    half = 9 * CH
    group = half // 3
    chunk1, chunk2 = group // n, group // n // n

    tm = lax.axis_index("tm")
    tile = lax.axis_index("tile")
    ntile = ny * 2
    z, x = lax.div(tm, nx), lax.rem(tm, nx)
    y, core = lax.div(tile, 2), lax.rem(tile, 2)

    def on_tm(d):
        return (lax.rem(tm + d, nt), tile)

    def axis_peer(axis, d):
        if axis == "x":
            return (z * nx + lax.rem(x + d, nx), tile)
        if axis == "z":
            return (lax.rem(z + d, nt // nx) * nx + x, tile)
        return (tm, lax.rem(y + d, ny) * 2 + core)

    where_on = {"x": x, "y": y, "z": z}
    mate = (tm, y * 2 + 1 - core)

    barrier = pltpu.get_barrier_semaphore()
    for d in range(1, nt):
        pl.semaphore_signal(barrier, inc=1, device_id=on_tm(d), device_id_type=MESH)
    for d in range(1, ntile):
        pl.semaphore_signal(
            barrier, inc=1, device_id=(tm, lax.rem(tile + d, ntile)), device_id_type=MESH
        )

    load_f = pltpu.make_async_copy(frames, F.at[:, pl.ds(1, R)], load_sem.at[0])
    load_c = pltpu.make_async_copy(cot, C.at[:, pl.ds(1, R)], load_sem.at[1])
    load_f.start()
    load_c.start()

    @pl.when(tile == 0)
    def _():
        for field in (F, C, S, I):
            field[:, 0] = jnp.zeros((T, W, CH), BF16)

    @pl.when(tile == ntile - 1)
    def _():
        for field in (F, C, S, I):
            field[:, R + 1] = jnp.zeros((T, W, CH), BF16)

    DEC[...] = jnp.exp(log_decay[...])
    whole = DEC[0:1, :]
    for t in range(1, T):
        whole = whole * DEC[t : t + 1, :]
    DG[tm] = jnp.broadcast_to(whole, (8, CH))

    for i in range(3):
        for j in range(3):
            rows = pl.ds((i * 3 + j) * CH, CH)
            from_rows = pl.ds(((2 - i) * 3 + 2 - j) * CH, CH)
            WOF[rows, :] = w_out[from_rows, :].T
            WIF[rows, :] = w_in[from_rows, :].T

    load_f.wait()
    load_c.wait()
    pl.semaphore_wait(barrier, nt - 1 + ntile - 1)

    def halo(field, k):
        up = pltpu.make_async_remote_copy(
            field.at[:, pl.ds(1, 1)], field.at[:, pl.ds(R + 1, 1)],
            halo_send.at[k, 0], halo_recv.at[k, 0],
            device_id=(tm, lax.max(tile - 1, 0)), device_id_type=MESH,
        )
        down = pltpu.make_async_remote_copy(
            field.at[:, pl.ds(R, 1)], field.at[:, pl.ds(0, 1)],
            halo_send.at[k, 1], halo_recv.at[k, 1],
            device_id=(tm, lax.min(tile + 1, ntile - 1)), device_id_type=MESH,
        )

        def start():
            @pl.when(tile > 0)
            def _():
                up.start()

            @pl.when(tile < ntile - 1)
            def _():
                down.start()

        def wait_recv():
            @pl.when(tile < ntile - 1)
            def _():
                up.wait_recv()

            @pl.when(tile > 0)
            def _():
                down.wait_recv()

        def wait_send():
            @pl.when(tile > 0)
            def _():
                up.wait_send()

            @pl.when(tile < ntile - 1)
            def _():
                down.wait_send()

        return start, wait_recv, wait_send

    halos = [halo(field, k) for k, field in enumerate((F, C, S, I))]
    halos[0][0]()
    halos[1][0]()
    for d in range(1, nt):
        pltpu.make_async_remote_copy(
            DG.at[tm], DG.at[tm], carry_send.at[0], carry_recv.at[0],
            device_id=on_tm(d), device_id_type=MESH,
        ).start()

    col = lax.broadcasted_iota(jnp.int32, (1, W, CH), 1)

    def widen(src, dst, rows):
        def one(t, _):
            for r0, count in rows:
                v = src[t, r0 : r0 + count].astype(F32)
                left = jnp.where(col == 0, 0.0, pltpu.roll(v, 1, 1))
                right = jnp.where(col == W - 1, 0.0, pltpu.roll(v, W - 1, 1))
                dst[t, r0 : r0 + count, :, 0:CH] = left.astype(BF16)
                dst[t, r0 : r0 + count, :, CH : 2 * CH] = src[t, r0 : r0 + count]
                dst[t, r0 : r0 + count, :, 2 * CH : 3 * CH] = right.astype(BF16)
            return 0

        lax.fori_loop(0, T, one, 0)

    inner = [(r, 1) for r in range(1, R + 1)]
    outer = [(0, 1), (R + 1, 1)]

    def taps(src3, t):
        return jnp.concatenate(
            [src3[t, i : i + R].reshape(pos, 3 * CH) for i in range(3)], axis=-1
        )

    def conv(src3, t, weight):
        return jnp.dot(taps(src3, t), weight[...], preferred_element_type=F32)

    widen(F, F3, inner)
    widen(C, C3, inner)
    halos[0][1]()
    halos[1][1]()
    widen(F, F3, outer)
    widen(C, C3, outer)

    for t in range(T):
        rate = DEC[t : t + 1, :]
        inflow = (1.0 - rate) * conv(F3, t, w_in)
        if t:
            inflow = rate * LS[t - 1] + inflow
        LS[t] = inflow

    def exchange(src_of, dst_of, k):
        for d in range(1, nt):
            peer = on_tm(d)
            pltpu.make_async_remote_copy(
                src_of(peer[0]), dst_of(peer[0]), carry_send.at[k], carry_recv.at[k],
                device_id=peer, device_id_type=MESH,
            ).start()

    def all_but_one(ref, k, sems):
        part = ref.at[pl.ds(0, nt - 1)]
        pltpu.make_async_copy(part, part, sems.at[k]).wait()

    def rows_of(ref, k):
        return ref.at[pl.ds(pl.multiple_of(k * piece, piece), piece)]

    mine = pl.ds(pl.multiple_of(tm * piece, piece), piece)
    exchange(lambda p: rows_of(LS.at[T - 1], p), lambda p: RF.at[tm], 1)
    RF[tm] = LS[T - 1, mine, :]

    for t in reversed(range(T)):
        adjoint = conv(C3, t, WOF)
        if t < T - 1:
            adjoint = adjoint + OB[...]
        LA[t] = adjoint
        OB[...] = DEC[t : t + 1, :] * adjoint
    exchange(lambda p: rows_of(OB, p), lambda p: RB.at[tm], 2)
    RB[tm] = OB[mine, :]

    all_but_one(DG, 0, carry_recv)
    all_but_one(RF, 1, carry_recv)
    carry = jnp.zeros((piece, CH), F32)
    for k in range(nt):
        EF[k] = carry
        carry = DG[k, 0:1, :] * carry + RF[k]
    exchange(lambda p: EF.at[p], lambda p: rows_of(INF, tm), 3)
    INF[mine, :] = EF[tm]

    all_but_one(RB, 2, carry_recv)
    carry = jnp.zeros((piece, CH), F32)
    for k in reversed(range(nt)):
        EB[k] = carry
        carry = DG[k, 0:1, :] * carry + RB[k]
    exchange(lambda p: EB.at[p], lambda p: rows_of(INB, tm), 4)
    INB[mine, :] = EB[tm]

    def arrived(ref, k):
        part = ref.at[pl.ds(0, (nt - 1) * piece)]
        pltpu.make_async_copy(part, part, carry_recv.at[k]).wait()

    arrived(INF, 3)
    reach = None
    for t in range(T):
        rate = DEC[t : t + 1, :]
        reach = rate if reach is None else reach * rate
        S[t, 1 : R + 1] = (LS[t] + reach * INF[...]).astype(BF16).reshape(R, W, CH)
    halos[2][0]()

    def gram(own, src3):
        total = jnp.zeros((CH, 9 * CH), F32)
        for t in range(T):
            total = total + lax.dot_general(
                own[t, 1 : R + 1].reshape(pos, CH), taps(src3, t),
                (((0,), (0,)), ((), ())), preferred_element_type=F32,
            )
        return total

    total = gram(S, C3)
    for i in range(3):
        for j in range(3):
            k = (2 - i) * 3 + 2 - j
            G[half + (i * 3 + j) * CH : half + (i * 3 + j + 1) * CH, :] = total[:, k * CH : (k + 1) * CH]

    arrived(INB, 4)
    tail = None
    for t in reversed(range(T)):
        rate = DEC[t : t + 1, :]
        adjoint = LA[t] + (INB[...] if tail is None else tail * INB[...])
        I[t, 1 : R + 1] = ((1.0 - rate) * adjoint).astype(BF16).reshape(R, W, CH)
        tail = rate if tail is None else tail * rate
    halos[3][0]()
    total = gram(I, F3)
    for k in range(9):
        G[k * CH : (k + 1) * CH, :] = total[:, k * CH : (k + 1) * CH].T

    def conv_out(which, t):
        if which == 0:
            src3, weight, field, stage, dst = S3, w_out, F, OB_F, output
        else:
            src3, weight, field, stage, dst = I3, WIF, C, OB_C, grad_frames
        direct = skip[...] * field[t, 1 : R + 1].reshape(pos, CH).astype(F32)
        stage[t] = (conv(src3, t, weight) + direct).astype(BF16).reshape(R, W, CH)
        pltpu.make_async_copy(stage.at[t], dst.at[t], out_sem.at[which, t]).start()

    def fill(k):
        if k == 0:
            widen(S, S3, inner)
            halos[2][1]()
            widen(S, S3, outer)
        elif k == 1:
            for t in range(T):
                conv_out(0, t)
        elif k == 2:
            widen(I, I3, inner)
        elif k == 3:
            halos[3][1]()
            widen(I, I3, outer)
        elif k == 4:
            for t in range(T):
                conv_out(1, t)

    own_half = pl.multiple_of(core * half, half)
    mate_half = pl.multiple_of((1 - core) * half, half)
    core_rs = pltpu.make_async_remote_copy(
        G.at[pl.ds(mate_half, half)], R0, ar_send.at[0], ar_recv.at[0],
        device_id=mate, device_id_type=MESH,
    )
    core_rs.start()
    fill(0)
    core_rs.wait_recv()

    orders = (("x", "y", "z"), ("y", "z", "x"), ("z", "x", "y"))

    def total_wait(ref, sem):
        pltpu.make_async_copy(ref, ref, sem).wait()

    def add_block(g):
        rows = pl.ds(pl.multiple_of(own_half + g * group, chunk1), group)
        G[rows, :] = G[rows, :] + R0[g * group : (g + 1) * group, :]

    for g in range(3):
        add_block(g)
        a = orders[g][0]
        for d in range(1, n):
            q = lax.rem(where_on[a] + d, n)
            pltpu.make_async_remote_copy(
                G.at[pl.ds(pl.multiple_of(own_half + g * group + q * chunk1, chunk1), chunk1)],
                R1.at[g, d - 1], ar_send.at[1], ar_recv.at[1 + g],
                device_id=axis_peer(a, d), device_id_type=MESH,
            ).start()
    fill(1)
    for g in range(3):
        total_wait(R1.at[g], ar_recv.at[1 + g])
        a, b = orders[g][:2]
        p = where_on[a]
        rows = pl.ds(pl.multiple_of(own_half + g * group + p * chunk1, chunk1), chunk1)
        value = G[rows, :]
        for d in range(n - 1):
            value = value + R1[g, d]
        O2[g] = value
        for d in range(1, n):
            q = lax.rem(where_on[b] + d, n)
            pltpu.make_async_remote_copy(
                O2.at[g, pl.ds(pl.multiple_of(q * chunk2, chunk2), chunk2)],
                R2.at[g, d - 1], ar_send.at[2], ar_recv.at[4 + g],
                device_id=axis_peer(b, d), device_id_type=MESH,
            ).start()
    fill(2)
    for g in range(3):
        total_wait(R2.at[g], ar_recv.at[4 + g])
        b, c = orders[g][1:]
        p = where_on[b]
        value = O2[g, pl.ds(pl.multiple_of(p * chunk2, chunk2), chunk2), :]
        for d in range(n - 1):
            value = value + R2[g, d]
        A2[g] = value * factor
        r = where_on[c]
        R3[g, r] = A2[g]
        for d in range(1, n):
            pltpu.make_async_remote_copy(
                A2.at[g], R3.at[g, r], ar_send.at[3], ar_recv.at[7 + g],
                device_id=axis_peer(c, d), device_id_type=MESH,
            ).start()
    fill(3)
    part = R2
    total_wait(part, ar_send.at[2])
    for g in range(3):
        total_wait(R3.at[g, pl.ds(0, n - 1)], ar_recv.at[7 + g])
        b = orders[g][1]
        value = R3[g, 0]
        for k in range(1, n):
            value = value + R3[g, k]
        p = where_on[b]
        A2_rows = pl.ds(pl.multiple_of(p * chunk2, chunk2), chunk2)
        O2[3 + g, A2_rows, :] = value
        for d in range(1, n):
            pltpu.make_async_remote_copy(
                O2.at[3 + g, A2_rows], O2.at[3 + g, A2_rows], ar_send.at[4], ar_recv.at[10 + g],
                device_id=axis_peer(b, d), device_id_type=MESH,
            ).start()
    fill(4)
    for g in range(3):
        total_wait(O2.at[3 + g, pl.ds(0, (n - 1) * chunk2)], ar_recv.at[10 + g])
        a = orders[g][0]
        p = where_on[a]
        rows = pl.ds(pl.multiple_of(own_half + g * group + p * chunk1, chunk1), chunk1)
        OUT[rows, :] = O2[3 + g]
        for d in range(1, n):
            pltpu.make_async_remote_copy(
                OUT.at[rows], OUT.at[rows], ar_send.at[5], ar_recv.at[13 + g],
                device_id=axis_peer(a, d), device_id_type=MESH,
            ).start()
    mate_copies = []
    for g in range(3):
        rows = pl.ds(pl.multiple_of(own_half + g * group, group), group)
        total_wait(OUT.at[pl.ds(0, (n - 1) * chunk1)], ar_recv.at[13 + g])
        mate_copies.append(pltpu.make_async_remote_copy(
            OUT.at[rows], OUT.at[rows], ar_send.at[6 + g], ar_recv.at[16 + g],
            device_id=mate, device_id_type=MESH,
        ))
        mate_copies[-1].start()
    for copy in mate_copies:
        copy.wait_recv()
    finals = [
        pltpu.make_async_copy(OUT.at[0:half], grad_in, out_sem.at[2, 0]),
        pltpu.make_async_copy(OUT.at[half : 2 * half], grad_out, out_sem.at[2, 1]),
    ]
    for copy in finals:
        copy.start()

    for copy in mate_copies:
        copy.wait_send()
    core_rs.wait_send()
    total_wait(R1, ar_send.at[1])
    total_wait(R3.at[:, pl.ds(0, n - 1)], ar_send.at[3])
    total_wait(R2, ar_send.at[4])
    total_wait(R1, ar_send.at[5])
    for k in range(4):
        halos[k][2]()
    all_but_one(DG, 0, carry_send)
    for k in range(1, 5):
        all_but_one(RF, k, carry_send)
    for t in range(T):
        pltpu.make_async_copy(OB_F.at[t], output.at[t], out_sem.at[0, t]).wait()
        pltpu.make_async_copy(OB_C.at[t], grad_frames.at[t], out_sem.at[1, t]).wait()
    for copy in finals:
        copy.wait()


def solution(mesh):
    nt, ntile = mesh.shape["tm"], mesh.shape["tile"]
    nx = math.isqrt(nt)
    ny = ntile // 2

    def step(frames, cot, w_in, w_out, skip, log_decay):
        T, R, W, CH = frames.shape
        factor = 1.0 / math.sqrt(T * nt * R * ntile * W)
        pos = R * W
        piece = pos // nt
        n = nx
        half = 9 * CH
        group = half // 3
        c1, c2 = group // n, group // n // n
        vm = pltpu.VMEM
        field = vm((T, R + 2, W, CH), BF16)
        field3 = vm((T, R + 2, W, 3 * CH), BF16)
        dma = pltpu.SemaphoreType.DMA
        anyspace = pl.BlockSpec(memory_space=pl.ANY)
        vmem = pl.BlockSpec(memory_space=pltpu.VMEM)
        res = pl.pallas_call(
            functools.partial(kernel, (nt, nx, ny, factor)),
            out_shape=(
                jax.ShapeDtypeStruct(frames.shape, BF16),
                jax.ShapeDtypeStruct(frames.shape, BF16),
                jax.ShapeDtypeStruct((half, CH), F32),
                jax.ShapeDtypeStruct((half, CH), F32),
            ),
            in_specs=[anyspace, anyspace, vmem, vmem, vmem, vmem],
            out_specs=[anyspace] * 4,
            scratch_shapes=[
                field, field, field, field,
                field3, field3, field3, field3,
                vm((half, CH), BF16), vm((half, CH), BF16),
                vm((T, pos, CH), F32), vm((T, pos, CH), F32), vm((pos, CH), F32),
                vm((T, CH), F32), vm((nt, 8, CH), F32),
                vm((nt, piece, CH), F32), vm((nt, piece, CH), F32), vm((pos, CH), F32),
                vm((nt, piece, CH), F32), vm((nt, piece, CH), F32), vm((pos, CH), F32),
                vm((2 * half, CH), F32), vm((half, CH), F32),
                vm((3, n - 1, c1, CH), F32), vm((3, n - 1, c2, CH), F32), vm((3, c2, CH), F32),
                vm((3, n, c2, CH), F32), vm((6, c1, CH), F32), vm((2 * half, CH), F32),
                vm((T, R, W, CH), BF16), vm((T, R, W, CH), BF16),
                dma((2,)), dma((4, 2)), dma((4, 2)), dma((5,)), dma((5,)),
                dma((9,)), dma((19,)), dma((3, T)),
            ],
            compiler_params=pltpu.CompilerParams(
                collective_id=0, has_side_effects=True, vmem_limit_bytes=60 * 2**20
            ),
        )(
            frames, cot, w_in.reshape(half, CH), w_out.reshape(half, CH),
            skip.reshape(1, CH), log_decay,
        )
        return (res[0], res[1], res[2].reshape(3, 3, CH, CH), res[3].reshape(3, 3, CH, CH))

    block = P("tm", "tile", None, None)
    return jax.shard_map(
        step,
        mesh=mesh,
        in_specs=(block, block, P(), P(), P(), P("tm", None)),
        out_specs=(block, block, P(), P()),
        check_vma=False,
    )
```

```python
import functools
import math

import jax
import jax.numpy as jnp
from jax import lax
from jax.experimental import pallas as pl
from jax.experimental.pallas import tpu as pltpu
from jax.sharding import PartitionSpec as P

MESH = pl.DeviceIdType.MESH
F32 = jnp.float32
BF16 = jnp.bfloat16
ROOT = 5


def encode(v):
    square = v * v
    return (v * (square * square)).astype(BF16)


def decode(code):
    w = code.astype(F32)
    root = jnp.exp2(jnp.log2(jnp.abs(w)) * (1.0 / ROOT))
    return jnp.where(w < 0.0, -root, root)


def chain_kernel(
    dims,
    frames, cot, w_in, w_out, skip, log_decay,
    own_out, mate_out, sums,
    X, Y, S, X3, Y3, S3, ST,
    WA, WB, COEF, DG,
    DR, LS, FIN, RF, EF, INC,
    G, GC, R1, R3, MO,
    load_sem, in_send, in_recv, halo_send, halo_recv,
    carry_send, carry_recv, fin_send, back_send, inc_recv, ar_send, ar_recv, mo_send, mo_recv,
):
    nt, nx, ny, factor = dims
    T, R, W, CH = frames.shape
    RC = 2 * R
    n = nx
    pos = RC * W
    half = 9 * CH
    group = half // 3
    chunk = group // (n * n)

    tm = lax.axis_index("tm")
    tile = lax.axis_index("tile")
    ntile = ny * 2
    z, x = lax.div(tm, nx), lax.rem(tm, nx)
    y, core = lax.div(tile, 2), lax.rem(tile, 2)
    forward = core == 1
    mate = (tm, y * 2 + 1 - core)

    def on_tm(d):
        return (lax.rem(tm + d, nt), tile)

    where_on = {"x": x, "y": y, "z": z}

    def axis_peer(axis, d):
        if axis == "x":
            return (z * nx + lax.rem(x + d, nx), tile)
        if axis == "z":
            return (lax.rem(z + d, nt // nx) * nx + x, tile)
        return (tm, lax.rem(y + d, ny) * 2 + core)

    def remote(src, dst, send, recv, device):
        return pltpu.make_async_remote_copy(
            src, dst, send, recv, device_id=device, device_id_type=MESH
        )

    def took(ref, sem):
        pltpu.make_async_copy(ref, ref, sem).wait()

    barrier = pltpu.get_barrier_semaphore()
    for d in range(1, nt):
        pl.semaphore_signal(barrier, inc=1, device_id=on_tm(d), device_id_type=MESH)
    for d in range(1, ntile):
        pl.semaphore_signal(
            barrier, inc=1, device_id=(tm, lax.rem(tile + d, ntile)), device_id_type=MESH
        )

    own_rows = pl.ds(1 + core * R, R)

    def load(first, second):
        pltpu.make_async_copy(first, X.at[:, own_rows], load_sem.at[0]).start()
        pltpu.make_async_copy(second, Y.at[:, own_rows], load_sem.at[1]).start()

    @pl.when(forward)
    def _():
        load(frames, cot)

    @pl.when(core == 0)
    def _():
        load(cot, frames)

    @pl.when(y == 0)
    def _():
        for field in (X, Y, S):
            field[:, 0] = jnp.zeros((T, W, CH), BF16)

    @pl.when(y == ny - 1)
    def _():
        for field in (X, Y, S):
            field[:, RC + 1] = jnp.zeros((T, W, CH), BF16)

    dec = jnp.exp(log_decay[...])
    whole = dec[0:1]
    for t in range(1, T):
        whole = whole * dec[t : t + 1]
    DG[tm] = jnp.broadcast_to(whole, (8, CH))
    one = jnp.ones((1, CH), F32)
    reach = None
    for i in range(T):
        a = jnp.where(forward, dec[i : i + 1], one if i == 0 else dec[T - i : T - i + 1])
        b = jnp.where(forward, 1.0 - dec[i : i + 1], one)
        c = jnp.where(forward, one, 1.0 - dec[T - 1 - i : T - i])
        reach = a if reach is None else reach * a
        COEF[i : i + 1] = a
        COEF[T + i : T + i + 1] = b
        COEF[2 * T + i : 2 * T + i + 1] = c
        COEF[3 * T + i : 3 * T + i + 1] = c * reach
    last = jnp.where(forward, one, dec[0:1])

    def weights(dst, plain, turned):
        @pl.when(forward)
        def _():
            dst[...] = plain[...]

        @pl.when(core == 0)
        def _():
            for k in range(9):
                dst[k * CH : (k + 1) * CH, :] = turned[(8 - k) * CH : (9 - k) * CH, :].T

    weights(WA, w_in, w_out)

    pl.semaphore_wait(barrier, nt - 1 + ntile - 1)

    def send_inputs(first, second):
        remote(first, X.at[:, own_rows], in_send.at[0], in_recv.at[0], mate).start()
        edge(0)
        remote(second, Y.at[:, own_rows], in_send.at[1], in_recv.at[1], mate).start()
        edge(1)

    edge_src = pl.ds(core * (R - 1), 1)
    edge_dst = pl.ds((1 - core) * (RC + 1), 1)
    next_y = y + 2 * core - 1
    has_next = (next_y >= 0) & (next_y < ny)
    safe_y = lax.min(lax.max(next_y, 0), ny - 1)

    def edge_copies(which):
        copies = []
        for c in range(2):
            src = (frames, cot)[(c == 1) == (which == 1)]
            dst = (X, Y)[which]
            copies.append(
                remote(
                    src.at[:, edge_src], dst.at[:, edge_dst],
                    halo_send.at[which, c], halo_recv.at[which, 1 - core],
                    (tm, safe_y * 2 + c),
                )
            )
        return copies

    def edge(which):
        @pl.when(has_next)
        def _():
            for copy in edge_copies(which):
                copy.start()

    @pl.when(forward)
    def _():
        send_inputs(cot, frames)

    @pl.when(core == 0)
    def _():
        send_inputs(frames, cot)

    for d in range(1, nt):
        remote(DG.at[tm], DG.at[tm], carry_send.at[0], carry_recv.at[0], on_tm(d)).start()

    def edge_took(which, field):
        @pl.when(y > 0)
        def _():
            took(field.at[:, pl.ds(0, 1)], halo_recv.at[which, 0])

        @pl.when(y < ny - 1)
        def _():
            took(field.at[:, pl.ds(RC + 1, 1)], halo_recv.at[which, 1])

    col = lax.broadcasted_iota(jnp.int32, (1, W, CH), 1)

    def widen(src, dst, row0, count):
        def step(k, _):
            r = row0 + k
            for t in range(T):
                v = src[t, pl.ds(r, 1)].astype(F32)
                left = jnp.where(col == 0, 0.0, pltpu.roll(v, 1, 1))
                right = jnp.where(col == W - 1, 0.0, pltpu.roll(v, W - 1, 1))
                dst[t, pl.ds(r, 1), :, 0:CH] = left.astype(BF16)
                dst[t, pl.ds(r, 1), :, CH : 2 * CH] = src[t, pl.ds(r, 1)]
                dst[t, pl.ds(r, 1), :, 2 * CH : 3 * CH] = right.astype(BF16)
            return 0

        lax.fori_loop(0, count, step, 0)

    def conv(src3, t, row0, count, weight):
        taps = jnp.concatenate(
            [src3[t, pl.ds(row0 + i, count)].reshape(count * W, 3 * CH) for i in range(3)], axis=-1
        )
        return jnp.dot(taps, weight[...], preferred_element_type=F32)

    def frame_of(i):
        return core * i + (1 - core) * (T - 1 - i)

    def local_scan(*spans):
        spans = [span for span in spans if span[1]]
        if not spans:
            return
        taps = jnp.concatenate(
            [
                jnp.concatenate([X3[:, pl.ds(row0 + i, count)] for row0, count in spans], axis=1)
                .reshape(-1, 3 * CH)
                for i in range(3)
            ],
            axis=-1,
        )
        drive = jnp.dot(taps, WA[...], preferred_element_type=F32)
        per_frame = drive.shape[0] // T
        for t in range(T):
            at = t * per_frame
            for row0, count in spans:
                rows = pl.ds(pl.multiple_of(row0 * W, W), count * W)
                DR[t, rows, :] = drive[at : at + count * W]
                at += count * W
        for row0, count in spans:
            rows = pl.ds(pl.multiple_of(row0 * W, W), count * W)
            for i in range(T):
                value = COEF[T + i : T + i + 1] * DR[frame_of(i), rows, :]
                if i:
                    value = value + COEF[i : i + 1] * LS[i - 1, rows, :]
                LS[i, rows, :] = value
            FIN[rows, :] = encode(last * value)
            send_finals(row0, count)

    def rows_of(ref, k):
        return ref.at[pl.ds(pl.multiple_of(k * W, W), W)]

    def send_finals(row0, count):
        for r in range(count):
            k = row0 + lax.rem(r + tm, count)

            @pl.when(k != tm)
            def _():
                remote(
                    rows_of(FIN, k), RF.at[tm], fin_send.at[k], carry_recv.at[1], (k, tile)
                ).start()

    took(X.at[:, pl.ds(1, R)], load_sem.at[0])
    widen(X, X3, 1 + core * R, R)
    local_scan((core * R + 1, R - 2))
    took(X.at[:, pl.ds(1, R)], in_recv.at[0])
    widen(X, X3, 1 + (1 - core) * R, R)
    if R > 2:
        local_scan(((1 - core) * (R - 1) + core, R))
    else:
        local_scan((1, RC - 2))
    edge_took(0, X)
    widen(X, X3, 0, 1)
    widen(X, X3, RC + 1, 1)
    local_scan((0, 1), (RC - 1, 1))

    others = pl.ds(0, nt - 1)
    RF[tm] = FIN[pl.ds(pl.multiple_of(tm * W, W), W), :]

    weights(WB, w_out, w_in)
    took(Y.at[:, pl.ds(1, R)], load_sem.at[1])
    took(Y.at[:, pl.ds(1, R)], in_recv.at[1])
    edge_took(1, Y)
    widen(Y, Y3, 0, RC + 2)

    took(DG.at[others], carry_recv.at[0])
    took(RF.at[others], carry_recv.at[1])
    carry = jnp.zeros((W, CH), F32)
    for i in range(nt):
        k = core * i + (1 - core) * (nt - 1 - i)
        EF[k] = encode(carry)

        @pl.when(k != tm)
        def _():
            remote(EF.at[k], rows_of(INC, tm), back_send.at[k], inc_recv.at[tm], (k, tile)).start()

        if i < nt - 1:
            carry = DG[k, 0:1, :] * carry + decode(RF[k])
    INC[pl.ds(pl.multiple_of(tm * W, W), W), :] = EF[tm]

    def finish(row0, count):
        for k in range(row0, row0 + count):

            @pl.when(tm != k)
            def _():
                took(rows_of(INC, k), inc_recv.at[k])

        rows = slice(row0 * W, (row0 + count) * W)
        incoming = decode(INC[rows, :])
        for i in range(T):
            value = (
                COEF[2 * T + i : 2 * T + i + 1] * LS[i, rows, :]
                + COEF[3 * T + i : 3 * T + i + 1] * incoming
            )
            S[frame_of(i), 1 + row0 : 1 + row0 + count] = value.astype(BF16).reshape(count, W, CH)

    finish(1, RC - 2)
    finish(0, 1)
    finish(RC - 1, 1)

    up = remote(
        S.at[:, pl.ds(1, 1)], S.at[:, pl.ds(RC + 1, 1)], halo_send.at[2, 0], halo_recv.at[2, 1],
        (tm, lax.max(y - 1, 0) * 2 + core),
    )
    down = remote(
        S.at[:, pl.ds(RC, 1)], S.at[:, pl.ds(0, 1)], halo_send.at[2, 1], halo_recv.at[2, 0],
        (tm, lax.min(y + 1, ny - 1) * 2 + core),
    )

    @pl.when(y > 0)
    def _():
        up.start()

    @pl.when(y < ny - 1)
    def _():
        down.start()

    orders = (("x", "y", "z"), ("y", "z", "x"), ("z", "x", "y"))
    steps = [(da, db) for da in range(n) for db in range(n) if da or db]
    steps.sort(key=lambda s: -sum(min(d, n - d) for d in s))

    def place(g, da, db):
        a, b = orders[g][:2]
        return lax.rem(where_on[a] + da, n) * n + lax.rem(where_on[b] + db, n)

    def plane_peer(g, da, db):
        at = dict(where_on)
        for axis, d in zip(orders[g], (da, db)):
            at[axis] = lax.rem(at[axis] + d, n)
        return (at["z"] * nx + at["x"], at["y"] * 2 + core)

    for t in range(T):
        ST[t] = S[t, 1 : RC + 1].reshape(pos, CH).T
    for g in range(3):
        first = core * (2 - g) + (1 - core) * g
        total = jnp.zeros((CH, 3 * CH), F32)
        for t in range(T):
            other = Y3[t, pl.ds(first, RC)].reshape(pos, 3 * CH)
            total = total + jnp.dot(ST[t], other, preferred_element_type=F32)
        total = total * factor

        @pl.when(forward)
        def _():
            for j in range(3):
                block = total[:, (2 - j) * CH : (3 - j) * CH]
                G[(g * 3 + j) * CH : (g * 3 + j + 1) * CH, :] = block
                GC[(g * 3 + j) * CH : (g * 3 + j + 1) * CH, :] = encode(block)

        @pl.when(core == 0)
        def _():
            for j in range(3):
                block = total[:, j * CH : (j + 1) * CH].T
                G[(g * 3 + j) * CH : (g * 3 + j + 1) * CH, :] = block
                GC[(g * 3 + j) * CH : (g * 3 + j + 1) * CH, :] = encode(block)

        for slot, (da, db) in enumerate(steps):
            q = place(g, da, db)
            remote(
                GC.at[pl.ds(pl.multiple_of(g * group + q * chunk, chunk), chunk)],
                R1.at[g, slot], ar_send.at[0], ar_recv.at[g], plane_peer(g, da, db),
            ).start()

    def conv_out(t):
        for side, (start, stage) in enumerate(((core * R, own_out), ((1 - core) * R, MO))):
            rows = pl.ds(start + 1, R)
            direct = skip[...] * X[t, rows].reshape(R * W, CH).astype(F32)
            value = conv(S3, t, start, R, WB) + direct
            stage[t] = value.astype(BF16).reshape(R, W, CH)
        remote(MO.at[t], mate_out.at[t], mo_send.at[t], mo_recv.at[t], mate).start()

    widen(S, S3, 1, RC)

    @pl.when(y > 0)
    def _():
        took(S.at[:, pl.ds(0, 1)], halo_recv.at[2, 0])

    @pl.when(y < ny - 1)
    def _():
        took(S.at[:, pl.ds(0, 1)], halo_recv.at[2, 1])

    widen(S, S3, 0, 1)
    widen(S, S3, RC + 1, 1)

    conv_out(0)
    conv_out(1)
    for g in range(3):
        took(R1.at[g], ar_recv.at[g])
        value = G[pl.ds(pl.multiple_of(g * group + place(g, 0, 0) * chunk, chunk), chunk), :]
        for slot in range(n * n - 1):
            value = value + decode(R1[g, slot])
        c = orders[g][2]
        r = where_on[c]
        R3[g, r] = value
        for d in range(1, n):
            remote(
                R3.at[g, r], R3.at[g, r], ar_send.at[1], ar_recv.at[3 + g], axis_peer(c, d)
            ).start()
    conv_out(2)
    base = core * half
    for g in range(3):
        took(R3.at[g, pl.ds(0, n - 1)], ar_recv.at[3 + g])
        value = R3[g, 0]
        for k in range(1, n):
            value = value + R3[g, k]
        rows = pl.ds(pl.multiple_of(base + g * group + place(g, 0, 0) * chunk, chunk), chunk)
        sums[rows, :] = value.astype(BF16)
        for da, db in steps:
            remote(
                sums.at[rows], sums.at[rows], ar_send.at[2], ar_recv.at[6 + g],
                plane_peer(g, da, db),
            ).start()
    conv_out(3)
    to_mate = []
    for g in range(3):
        rows = pl.ds(pl.multiple_of(base + g * group, group), group)
        took(sums.at[pl.ds(0, group - chunk)], ar_recv.at[6 + g])
        to_mate.append(
            remote(sums.at[rows], sums.at[rows], ar_send.at[3 + g], ar_recv.at[9 + g], mate)
        )
        to_mate[-1].start()

    for t in range(T):
        took(MO.at[t], mo_recv.at[t])
    for copy in to_mate:
        copy.wait_recv()

    for copy in to_mate:
        copy.wait_send()
    for t in range(T):
        took(MO.at[t], mo_send.at[t])
    took(R1, ar_send.at[0])
    took(R3.at[:, pl.ds(0, n - 1)], ar_send.at[1])
    took(sums.at[pl.ds(0, half - 3 * chunk)], ar_send.at[2])
    took(DG.at[others], carry_send.at[0])
    for k in range(nt):

        @pl.when(tm != k)
        def _():
            took(EF.at[0], fin_send.at[k])
            took(EF.at[0], back_send.at[k])

    for k in range(2):
        took(X.at[:, pl.ds(1, R)], in_send.at[k])

    @pl.when(has_next)
    def _():
        for which in range(2):
            for copy in edge_copies(which):
                copy.wait_send()

    @pl.when(y > 0)
    def _():
        up.wait_send()

    @pl.when(y < ny - 1)
    def _():
        down.wait_send()


def store_kernel(own_out, mate_out, sums, output, grad_frames, grad_in, grad_out, wide, sem):
    forward = lax.rem(lax.axis_index("tile"), 2) == 1
    half = grad_in.shape[0]

    def put(first, second):
        pltpu.make_async_copy(own_out, first, sem.at[0]).start()
        pltpu.make_async_copy(mate_out, second, sem.at[1]).start()

    @pl.when(forward)
    def _():
        put(output, grad_frames)

    @pl.when(jnp.logical_not(forward))
    def _():
        put(grad_frames, output)

    copies = []
    for k, dst in enumerate((grad_in, grad_out)):
        wide[k] = sums[k * half : (k + 1) * half, :].astype(F32)
        copies.append(pltpu.make_async_copy(wide.at[k], dst, sem.at[2 + k]))
        copies[-1].start()
    pltpu.make_async_copy(own_out, output, sem.at[0]).wait()
    pltpu.make_async_copy(mate_out, grad_frames, sem.at[1]).wait()
    for copy in copies:
        copy.wait()


def solution(mesh):
    nt, ntile = mesh.shape["tm"], mesh.shape["tile"]
    nx = math.isqrt(nt)
    ny = ntile // 2

    def step(frames, cot, w_in, w_out, skip, log_decay):
        T, R, W, CH = frames.shape
        factor = 1.0 / math.sqrt(T * nt * R * ntile * W)
        RC = 2 * R
        pos = RC * W
        n = nx
        half = 9 * CH
        chunk = half // 3 // (n * n)
        vm = pltpu.VMEM
        field = vm((T, RC + 2, W, CH), BF16)
        field3 = vm((T, RC + 2, W, 3 * CH), BF16)
        dma = pltpu.SemaphoreType.DMA
        hbm = pl.BlockSpec(memory_space=pl.ANY)
        vmem = pl.BlockSpec(memory_space=pltpu.VMEM)
        own_out, mate_out, sums = pl.pallas_call(
            functools.partial(chain_kernel, (nt, nx, ny, factor)),
            out_shape=(
                vm(frames.shape, BF16),
                vm(frames.shape, BF16),
                vm((2 * half, CH), BF16),
            ),
            in_specs=[hbm, hbm, vmem, vmem, vmem, vmem],
            out_specs=[vmem] * 3,
            scratch_shapes=[
                field, field, field, field3, field3, field3, vm((T, CH, pos), BF16),
                vm((half, CH), BF16), vm((half, CH), BF16), vm((4 * T, CH), F32), vm((nt, 8, CH), F32),
                vm((T, pos, CH), F32), vm((T, pos, CH), F32), vm((pos, CH), BF16),
                vm((nt, W, CH), BF16), vm((nt, W, CH), BF16), vm((pos, CH), BF16),
                vm((half, CH), F32), vm((half, CH), BF16),
                vm((3, n * n - 1, chunk, CH), BF16), vm((3, n, chunk, CH), F32), vm(frames.shape, BF16),
                dma((2,)), dma((2,)), dma((2,)), dma((3, 2)), dma((3, 2)),
                dma((1,)), dma((2,)), dma((nt,)), dma((nt,)), dma((nt,)),
                dma((6,)), dma((12,)), dma((T,)), dma((T,)),
            ],
            compiler_params=pltpu.CompilerParams(
                collective_id=0, has_side_effects=True, vmem_limit_bytes=65_300_000
            ),
        )(
            frames, cot, w_in.reshape(half, CH), w_out.reshape(half, CH),
            skip.reshape(1, CH), log_decay,
        )
        res = pl.pallas_call(
            store_kernel,
            out_shape=(
                jax.ShapeDtypeStruct(frames.shape, BF16),
                jax.ShapeDtypeStruct(frames.shape, BF16),
                jax.ShapeDtypeStruct((half, CH), F32),
                jax.ShapeDtypeStruct((half, CH), F32),
            ),
            in_specs=[vmem] * 3,
            out_specs=[hbm] * 4,
            scratch_shapes=[vm((2, half, CH), F32), dma((4,))],
            compiler_params=pltpu.CompilerParams(vmem_limit_bytes=8 * 2**20),
        )(own_out, mate_out, sums)
        return (res[0], res[1], res[2].reshape(3, 3, CH, CH), res[3].reshape(3, 3, CH, CH))

    block = P("tm", "tile", None, None)
    return jax.shard_map(
        step,
        mesh=mesh,
        in_specs=(block, block, P(), P(), P(), P("tm", None)),
        out_specs=(block, block, P(), P()),
        check_vma=False,
    )
```

```python
import functools
import math

import jax
import jax.numpy as jnp
from jax import lax
from jax.experimental import pallas as pl
from jax.experimental.pallas import tpu as pltpu
from jax.sharding import PartitionSpec as P

MESH = pl.DeviceIdType.MESH
F32 = jnp.float32
BF16 = jnp.bfloat16
ROOT = 5


def encode(v):
    square = v * v
    return (v * (square * square)).astype(BF16)


def decode(code):
    w = code.astype(F32)
    root = jnp.exp2(jnp.log2(jnp.abs(w)) * (1.0 / ROOT))
    return jnp.where(w < 0.0, -root, root)


def chain_kernel(
    dims,
    frames, cot, w_in, w_out, skip, log_decay,
    own_out, mate_out, sums,
    X, Y, S, X3, Y3, S3, ST,
    WA, WB, COEF, DG,
    DR, LS, FIN, RF, EF, INC,
    G, GC, R1, R3, MO,
    load_sem, in_send, in_recv, halo_send, halo_recv,
    carry_send, carry_recv, fin_send, back_send, inc_recv, ar_send, ar_recv, mo_send, mo_recv, round_sem,
):
    nt, nx, ny, factor = dims
    T, R, W, CH = frames.shape
    RC = 2 * R
    n = nx
    pos = RC * W
    half = 9 * CH
    group = half // 3
    chunk = group // (n * n)

    tm = lax.axis_index("tm")
    tile = lax.axis_index("tile")
    ntile = ny * 2
    z, x = lax.div(tm, nx), lax.rem(tm, nx)
    y, core = lax.div(tile, 2), lax.rem(tile, 2)
    forward = core == 1
    mate = (tm, y * 2 + 1 - core)

    def on_tm(d):
        return (lax.rem(tm + d, nt), tile)

    where_on = {"x": x, "y": y, "z": z}

    def axis_peer(axis, d):
        if axis == "x":
            return (z * nx + lax.rem(x + d, nx), tile)
        if axis == "z":
            return (lax.rem(z + d, nt // nx) * nx + x, tile)
        return (tm, lax.rem(y + d, ny) * 2 + core)

    def remote(src, dst, send, recv, device):
        return pltpu.make_async_remote_copy(
            src, dst, send, recv, device_id=device, device_id_type=MESH
        )

    def took(ref, sem):
        pltpu.make_async_copy(ref, ref, sem).wait()

    near = [axis_peer(axis, d) for axis in ("x", "y", "z") for d in (1, n - 1)]
    across = [(tm, lax.rem(y + d, ny) * 2 + 1 - core) for d in (1, ny - 1)]
    barrier = pltpu.get_barrier_semaphore()
    for device in [mate, *near, *across]:
        pl.semaphore_signal(barrier, inc=1, device_id=device, device_id_type=MESH)

    def greet(k):
        for device in near:
            pl.semaphore_signal(round_sem.at[k], inc=1, device_id=device, device_id_type=MESH)

    def greeted(k):
        pl.semaphore_wait(round_sem.at[k], len(near))

    own_rows = pl.ds(1 + core * R, R)

    def load(first, second):
        pltpu.make_async_copy(first, X.at[:, own_rows], load_sem.at[0]).start()
        pltpu.make_async_copy(second, Y.at[:, own_rows], load_sem.at[1]).start()

    @pl.when(forward)
    def _():
        load(frames, cot)

    @pl.when(core == 0)
    def _():
        load(cot, frames)

    @pl.when(y == 0)
    def _():
        for field in (X, Y, S):
            field[:, 0] = jnp.zeros((T, W, CH), BF16)

    @pl.when(y == ny - 1)
    def _():
        for field in (X, Y, S):
            field[:, RC + 1] = jnp.zeros((T, W, CH), BF16)

    dec = jnp.exp(log_decay[...])
    whole = dec[0:1]
    for t in range(1, T):
        whole = whole * dec[t : t + 1]
    DG[tm] = jnp.broadcast_to(whole, (8, CH))
    one = jnp.ones((1, CH), F32)
    reach = None
    for i in range(T):
        a = jnp.where(forward, dec[i : i + 1], one if i == 0 else dec[T - i : T - i + 1])
        b = jnp.where(forward, 1.0 - dec[i : i + 1], one)
        c = jnp.where(forward, one, 1.0 - dec[T - 1 - i : T - i])
        reach = a if reach is None else reach * a
        COEF[i : i + 1] = a
        COEF[T + i : T + i + 1] = b
        COEF[2 * T + i : 2 * T + i + 1] = c
        COEF[3 * T + i : 3 * T + i + 1] = c * reach
    last = jnp.where(forward, one, dec[0:1])

    def weights(dst, plain, turned):
        @pl.when(forward)
        def _():
            dst[...] = plain[...]

        @pl.when(core == 0)
        def _():
            for k in range(9):
                dst[k * CH : (k + 1) * CH, :] = turned[(8 - k) * CH : (9 - k) * CH, :].T

    weights(WA, w_in, w_out)

    pl.semaphore_wait(barrier, 1 + len(near) + len(across))

    def send_inputs(first, second):
        remote(first, X.at[:, own_rows], in_send.at[0], in_recv.at[0], mate).start()
        edge(0)
        remote(second, Y.at[:, own_rows], in_send.at[1], in_recv.at[1], mate).start()
        edge(1)

    edge_src = pl.ds(core * (R - 1), 1)
    edge_dst = pl.ds((1 - core) * (RC + 1), 1)
    next_y = y + 2 * core - 1
    has_next = (next_y >= 0) & (next_y < ny)
    safe_y = lax.min(lax.max(next_y, 0), ny - 1)

    def edge_copies(which):
        copies = []
        for c in range(2):
            src = (frames, cot)[(c == 1) == (which == 1)]
            dst = (X, Y)[which]
            copies.append(
                remote(
                    src.at[:, edge_src], dst.at[:, edge_dst],
                    halo_send.at[which, c], halo_recv.at[which, 1 - core],
                    (tm, safe_y * 2 + c),
                )
            )
        return copies

    def edge(which):
        @pl.when(has_next)
        def _():
            for copy in edge_copies(which):
                copy.start()

    @pl.when(forward)
    def _():
        send_inputs(cot, frames)

    @pl.when(core == 0)
    def _():
        send_inputs(frames, cot)

    greet(0)

    def edge_took(which, field):
        @pl.when(y > 0)
        def _():
            took(field.at[:, pl.ds(0, 1)], halo_recv.at[which, 0])

        @pl.when(y < ny - 1)
        def _():
            took(field.at[:, pl.ds(RC + 1, 1)], halo_recv.at[which, 1])

    col = lax.broadcasted_iota(jnp.int32, (1, W, CH), 1)

    def widen(src, dst, row0, count):
        def step(k, _):
            r = row0 + k
            for t in range(T):
                v = src[t, pl.ds(r, 1)].astype(F32)
                left = jnp.where(col == 0, 0.0, pltpu.roll(v, 1, 1))
                right = jnp.where(col == W - 1, 0.0, pltpu.roll(v, W - 1, 1))
                dst[t, pl.ds(r, 1), :, 0:CH] = left.astype(BF16)
                dst[t, pl.ds(r, 1), :, CH : 2 * CH] = src[t, pl.ds(r, 1)]
                dst[t, pl.ds(r, 1), :, 2 * CH : 3 * CH] = right.astype(BF16)
            return 0

        lax.fori_loop(0, count, step, 0)

    def conv(src3, t, row0, count, weight):
        taps = jnp.concatenate(
            [src3[t, pl.ds(row0 + i, count)].reshape(count * W, 3 * CH) for i in range(3)], axis=-1
        )
        return jnp.dot(taps, weight[...], preferred_element_type=F32)

    def frame_of(i):
        return core * i + (1 - core) * (T - 1 - i)

    def local_scan(*spans):
        spans = [span for span in spans if span[1]]
        if not spans:
            return
        taps = jnp.concatenate(
            [
                jnp.concatenate([X3[:, pl.ds(row0 + i, count)] for row0, count in spans], axis=1)
                .reshape(-1, 3 * CH)
                for i in range(3)
            ],
            axis=-1,
        )
        drive = jnp.dot(taps, WA[...], preferred_element_type=F32)
        per_frame = drive.shape[0] // T
        for t in range(T):
            at = t * per_frame
            for row0, count in spans:
                rows = pl.ds(pl.multiple_of(row0 * W, W), count * W)
                DR[t, rows, :] = drive[at : at + count * W]
                at += count * W
        for row0, count in spans:
            rows = pl.ds(pl.multiple_of(row0 * W, W), count * W)
            for i in range(T):
                value = COEF[T + i : T + i + 1] * DR[frame_of(i), rows, :]
                if i:
                    value = value + COEF[i : i + 1] * LS[i - 1, rows, :]
                LS[i, rows, :] = value
            FIN[rows, :] = encode(last * value)

    def rows_of(ref, k):
        return ref.at[pl.ds(pl.multiple_of(k * W, W), W)]

    def send_finals(row0, count):
        for r in range(count):
            k = row0 + lax.rem(r + tm, count)

            @pl.when(k != tm)
            def _():
                remote(
                    rows_of(FIN, k), RF.at[tm], fin_send.at[k], carry_recv.at[1], (k, tile)
                ).start()

    took(X.at[:, pl.ds(1, R)], load_sem.at[0])
    widen(X, X3, 1 + core * R, R)
    greeted(0)
    greet(1)
    local_scan((core * R + 1, R - 2))
    greeted(1)
    greet(2)
    took(X.at[:, pl.ds(1, R)], in_recv.at[0])
    widen(X, X3, 1 + (1 - core) * R, R)
    local_scan(((1 - core) * (R - 1) + core, R) if R > 2 else (1, RC - 2))
    greeted(2)
    send_finals(1, RC - 2)
    for d in range(1, nt):
        remote(DG.at[tm], DG.at[tm], carry_send.at[0], carry_recv.at[0], on_tm(d)).start()
    edge_took(0, X)
    widen(X, X3, 0, 1)
    widen(X, X3, RC + 1, 1)
    local_scan((0, 1), (RC - 1, 1))
    send_finals(0, 1)
    send_finals(RC - 1, 1)

    others = pl.ds(0, nt - 1)
    RF[tm] = FIN[pl.ds(pl.multiple_of(tm * W, W), W), :]

    weights(WB, w_out, w_in)
    took(Y.at[:, pl.ds(1, R)], load_sem.at[1])
    took(Y.at[:, pl.ds(1, R)], in_recv.at[1])
    edge_took(1, Y)
    widen(Y, Y3, 0, RC + 2)

    took(DG.at[others], carry_recv.at[0])
    took(RF.at[others], carry_recv.at[1])
    carry = jnp.zeros((W, CH), F32)
    for i in range(nt):
        k = core * i + (1 - core) * (nt - 1 - i)
        EF[k] = encode(carry)

        @pl.when(k != tm)
        def _():
            remote(EF.at[k], rows_of(INC, tm), back_send.at[k], inc_recv.at[tm], (k, tile)).start()

        if i < nt - 1:
            carry = DG[k, 0:1, :] * carry + decode(RF[k])
    INC[pl.ds(pl.multiple_of(tm * W, W), W), :] = EF[tm]

    def finish(row0, count):
        for k in range(row0, row0 + count):

            @pl.when(tm != k)
            def _():
                took(rows_of(INC, k), inc_recv.at[k])

        rows = slice(row0 * W, (row0 + count) * W)
        incoming = decode(INC[rows, :])
        for i in range(T):
            value = (
                COEF[2 * T + i : 2 * T + i + 1] * LS[i, rows, :]
                + COEF[3 * T + i : 3 * T + i + 1] * incoming
            )
            S[frame_of(i), 1 + row0 : 1 + row0 + count] = value.astype(BF16).reshape(count, W, CH)

    finish(1, RC - 2)
    finish(0, 1)
    finish(RC - 1, 1)

    up = remote(
        S.at[:, pl.ds(1, 1)], S.at[:, pl.ds(RC + 1, 1)], halo_send.at[2, 0], halo_recv.at[2, 1],
        (tm, lax.max(y - 1, 0) * 2 + core),
    )
    down = remote(
        S.at[:, pl.ds(RC, 1)], S.at[:, pl.ds(0, 1)], halo_send.at[2, 1], halo_recv.at[2, 0],
        (tm, lax.min(y + 1, ny - 1) * 2 + core),
    )

    @pl.when(y > 0)
    def _():
        up.start()

    @pl.when(y < ny - 1)
    def _():
        down.start()

    orders = (("x", "y", "z"), ("y", "z", "x"), ("z", "x", "y"))
    steps = [(da, db) for da in range(n) for db in range(n) if da or db]
    steps.sort(key=lambda s: -sum(min(d, n - d) for d in s))

    def place(g, da, db):
        a, b = orders[g][:2]
        return lax.rem(where_on[a] + da, n) * n + lax.rem(where_on[b] + db, n)

    def plane_peer(g, da, db):
        at = dict(where_on)
        for axis, d in zip(orders[g], (da, db)):
            at[axis] = lax.rem(at[axis] + d, n)
        return (at["z"] * nx + at["x"], at["y"] * 2 + core)

    for t in range(T):
        ST[t] = S[t, 1 : RC + 1].reshape(pos, CH).T
    for g in range(3):
        first = core * (2 - g) + (1 - core) * g
        total = jnp.zeros((CH, 3 * CH), F32)
        for t in range(T):
            other = Y3[t, pl.ds(first, RC)].reshape(pos, 3 * CH)
            total = total + jnp.dot(ST[t], other, preferred_element_type=F32)
        total = total * factor

        @pl.when(forward)
        def _():
            for j in range(3):
                block = total[:, (2 - j) * CH : (3 - j) * CH]
                G[(g * 3 + j) * CH : (g * 3 + j + 1) * CH, :] = block
                GC[(g * 3 + j) * CH : (g * 3 + j + 1) * CH, :] = encode(block)

        @pl.when(core == 0)
        def _():
            for j in range(3):
                block = total[:, j * CH : (j + 1) * CH].T
                G[(g * 3 + j) * CH : (g * 3 + j + 1) * CH, :] = block
                GC[(g * 3 + j) * CH : (g * 3 + j + 1) * CH, :] = encode(block)

        for slot, (da, db) in enumerate(steps):
            q = place(g, da, db)
            remote(
                GC.at[pl.ds(pl.multiple_of(g * group + q * chunk, chunk), chunk)],
                R1.at[g, slot], ar_send.at[0], ar_recv.at[g], plane_peer(g, da, db),
            ).start()

    def conv_out(t):
        for side, (start, stage) in enumerate(((core * R, own_out), ((1 - core) * R, MO))):
            rows = pl.ds(start + 1, R)
            direct = skip[...] * X[t, rows].reshape(R * W, CH).astype(F32)
            value = conv(S3, t, start, R, WB) + direct
            stage[t] = value.astype(BF16).reshape(R, W, CH)
        remote(MO.at[t], mate_out.at[t], mo_send.at[t], mo_recv.at[t], mate).start()

    widen(S, S3, 1, RC)

    @pl.when(y > 0)
    def _():
        took(S.at[:, pl.ds(0, 1)], halo_recv.at[2, 0])

    @pl.when(y < ny - 1)
    def _():
        took(S.at[:, pl.ds(0, 1)], halo_recv.at[2, 1])

    widen(S, S3, 0, 1)
    widen(S, S3, RC + 1, 1)

    conv_out(0)
    conv_out(1)
    for g in range(3):
        took(R1.at[g], ar_recv.at[g])
        value = G[pl.ds(pl.multiple_of(g * group + place(g, 0, 0) * chunk, chunk), chunk), :]
        for slot in range(n * n - 1):
            value = value + decode(R1[g, slot])
        c = orders[g][2]
        r = where_on[c]
        R3[g, r] = value
        for d in range(1, n):
            remote(
                R3.at[g, r], R3.at[g, r], ar_send.at[1], ar_recv.at[3 + g], axis_peer(c, d)
            ).start()
    conv_out(2)
    base = core * half
    for g in range(3):
        took(R3.at[g, pl.ds(0, n - 1)], ar_recv.at[3 + g])
        value = R3[g, 0]
        for k in range(1, n):
            value = value + R3[g, k]
        rows = pl.ds(pl.multiple_of(base + g * group + place(g, 0, 0) * chunk, chunk), chunk)
        sums[rows, :] = value.astype(BF16)
        for da, db in steps:
            remote(
                sums.at[rows], sums.at[rows], ar_send.at[2], ar_recv.at[6 + g],
                plane_peer(g, da, db),
            ).start()
    conv_out(3)
    to_mate = []
    for g in range(3):
        rows = pl.ds(pl.multiple_of(base + g * group, group), group)
        took(sums.at[pl.ds(0, group - chunk)], ar_recv.at[6 + g])
        to_mate.append(
            remote(sums.at[rows], sums.at[rows], ar_send.at[3 + g], ar_recv.at[9 + g], mate)
        )
        to_mate[-1].start()

    for t in range(T):
        took(MO.at[t], mo_recv.at[t])
    for copy in to_mate:
        copy.wait_recv()

    for copy in to_mate:
        copy.wait_send()
    for t in range(T):
        took(MO.at[t], mo_send.at[t])
    took(R1, ar_send.at[0])
    took(R3.at[:, pl.ds(0, n - 1)], ar_send.at[1])
    took(sums.at[pl.ds(0, half - 3 * chunk)], ar_send.at[2])
    took(DG.at[others], carry_send.at[0])
    for k in range(nt):

        @pl.when(tm != k)
        def _():
            took(EF.at[0], fin_send.at[k])
            took(EF.at[0], back_send.at[k])

    for k in range(2):
        took(X.at[:, pl.ds(1, R)], in_send.at[k])

    @pl.when(has_next)
    def _():
        for which in range(2):
            for copy in edge_copies(which):
                copy.wait_send()

    @pl.when(y > 0)
    def _():
        up.wait_send()

    @pl.when(y < ny - 1)
    def _():
        down.wait_send()


def store_kernel(own_out, mate_out, sums, output, grad_frames, grad_in, grad_out, wide, sem):
    forward = lax.rem(lax.axis_index("tile"), 2) == 1
    half = grad_in.shape[0]

    def put(first, second):
        pltpu.make_async_copy(own_out, first, sem.at[0]).start()
        pltpu.make_async_copy(mate_out, second, sem.at[1]).start()

    @pl.when(forward)
    def _():
        put(output, grad_frames)

    @pl.when(jnp.logical_not(forward))
    def _():
        put(grad_frames, output)

    copies = []
    for k, dst in enumerate((grad_in, grad_out)):
        wide[k] = sums[k * half : (k + 1) * half, :].astype(F32)
        copies.append(pltpu.make_async_copy(wide.at[k], dst, sem.at[2 + k]))
        copies[-1].start()
    pltpu.make_async_copy(own_out, output, sem.at[0]).wait()
    pltpu.make_async_copy(mate_out, grad_frames, sem.at[1]).wait()
    for copy in copies:
        copy.wait()


def solution(mesh):
    nt, ntile = mesh.shape["tm"], mesh.shape["tile"]
    nx = math.isqrt(nt)
    ny = ntile // 2

    def step(frames, cot, w_in, w_out, skip, log_decay):
        T, R, W, CH = frames.shape
        factor = 1.0 / math.sqrt(T * nt * R * ntile * W)
        RC = 2 * R
        pos = RC * W
        n = nx
        half = 9 * CH
        chunk = half // 3 // (n * n)
        vm = pltpu.VMEM
        field = vm((T, RC + 2, W, CH), BF16)
        field3 = vm((T, RC + 2, W, 3 * CH), BF16)
        dma = pltpu.SemaphoreType.DMA
        hbm = pl.BlockSpec(memory_space=pl.ANY)
        vmem = pl.BlockSpec(memory_space=pltpu.VMEM)
        own_out, mate_out, sums = pl.pallas_call(
            functools.partial(chain_kernel, (nt, nx, ny, factor)),
            out_shape=(
                vm(frames.shape, BF16),
                vm(frames.shape, BF16),
                vm((2 * half, CH), BF16),
            ),
            in_specs=[hbm, hbm, vmem, vmem, vmem, vmem],
            out_specs=[vmem] * 3,
            scratch_shapes=[
                field, field, field, field3, field3, field3, vm((T, CH, pos), BF16),
                vm((half, CH), BF16), vm((half, CH), BF16), vm((4 * T, CH), F32), vm((nt, 8, CH), F32),
                vm((T, pos, CH), F32), vm((T, pos, CH), F32), vm((pos, CH), BF16),
                vm((nt, W, CH), BF16), vm((nt, W, CH), BF16), vm((pos, CH), BF16),
                vm((half, CH), F32), vm((half, CH), BF16),
                vm((3, n * n - 1, chunk, CH), BF16), vm((3, n, chunk, CH), F32), vm(frames.shape, BF16),
                dma((2,)), dma((2,)), dma((2,)), dma((3, 2)), dma((3, 2)),
                dma((1,)), dma((2,)), dma((nt,)), dma((nt,)), dma((nt,)),
                dma((6,)), dma((12,)), dma((T,)), dma((T,)),
                pltpu.SemaphoreType.REGULAR((3,)),
            ],
            compiler_params=pltpu.CompilerParams(
                collective_id=0, has_side_effects=True, vmem_limit_bytes=65_300_000
            ),
        )(
            frames, cot, w_in.reshape(half, CH), w_out.reshape(half, CH),
            skip.reshape(1, CH), log_decay,
        )
        res = pl.pallas_call(
            store_kernel,
            out_shape=(
                jax.ShapeDtypeStruct(frames.shape, BF16),
                jax.ShapeDtypeStruct(frames.shape, BF16),
                jax.ShapeDtypeStruct((half, CH), F32),
                jax.ShapeDtypeStruct((half, CH), F32),
            ),
            in_specs=[vmem] * 3,
            out_specs=[hbm] * 4,
            scratch_shapes=[vm((2, half, CH), F32), dma((4,))],
            compiler_params=pltpu.CompilerParams(vmem_limit_bytes=8 * 2**20),
        )(own_out, mate_out, sums)
        return (res[0], res[1], res[2].reshape(3, 3, CH, CH), res[3].reshape(3, 3, CH, CH))

    block = P("tm", "tile", None, None)
    return jax.shard_map(
        step,
        mesh=mesh,
        in_specs=(block, block, P(), P(), P(), P("tm", None)),
        out_specs=(block, block, P(), P()),
        check_vma=False,
    )
```

```python
import functools
import math

import jax
import jax.numpy as jnp
from jax import lax
from jax.experimental import pallas as pl
from jax.experimental.pallas import tpu as pltpu
from jax.sharding import PartitionSpec as P

MESH = pl.DeviceIdType.MESH
F32 = jnp.float32
BF16 = jnp.bfloat16
ROOT = 5


def encode(v):
    square = v * v
    return (v * (square * square)).astype(BF16)


def decode(code):
    w = code.astype(F32)
    root = jnp.exp2(jnp.log2(jnp.abs(w)) * (1.0 / ROOT))
    return jnp.where(w < 0.0, -root, root)


def chain_kernel(
    dims,
    frames, cot, w_in_hbm, w_out_hbm, skip_hbm, log_decay_hbm,
    own_out, mate_out, sums,
    X, Y, S, X3, Y3, S3, ST,
    w_in, w_out, skip, log_decay, WA, WB, COEF, DG,
    DR, LS, LST, FIN, RF, EF, INC,
    G, GC, R1, R3, MO,
    load_sem, in_send, in_recv, halo_send, halo_recv,
    carry_send, carry_recv, fin_send, back_send, inc_recv, ar_send, ar_recv, mo_send, mo_recv,
):
    nt, nx, ny, factor = dims
    T, R, W, CH = frames.shape
    RC = 2 * R
    n = nx
    pos = RC * W
    half = 9 * CH
    group = half // 3
    chunk = group // (n * n)

    tm = lax.axis_index("tm")
    tile = lax.axis_index("tile")
    ntile = ny * 2
    z, x = lax.div(tm, nx), lax.rem(tm, nx)
    y, core = lax.div(tile, 2), lax.rem(tile, 2)
    forward = core == 1
    mate = (tm, y * 2 + 1 - core)

    def on_tm(d):
        return (lax.rem(tm + d, nt), tile)

    where_on = {"x": x, "y": y, "z": z}

    def axis_peer(axis, d):
        if axis == "x":
            return (z * nx + lax.rem(x + d, nx), tile)
        if axis == "z":
            return (lax.rem(z + d, nt // nx) * nx + x, tile)
        return (tm, lax.rem(y + d, ny) * 2 + core)

    def remote(src, dst, send, recv, device):
        return pltpu.make_async_remote_copy(
            src, dst, send, recv, device_id=device, device_id_type=MESH
        )

    def took(ref, sem):
        pltpu.make_async_copy(ref, ref, sem).wait()

    barrier = pltpu.get_barrier_semaphore()
    for d in range(1, nt):
        pl.semaphore_signal(barrier, inc=1, device_id=on_tm(d), device_id_type=MESH)
    for d in range(1, ntile):
        pl.semaphore_signal(
            barrier, inc=1, device_id=(tm, lax.rem(tile + d, ntile)), device_id_type=MESH
        )

    own_rows = pl.ds(1 + core * R, R)
    small = [
        pltpu.make_async_copy(src, dst, load_sem.at[2 + k])
        for k, (src, dst) in enumerate(
            (
                (log_decay_hbm, log_decay), (w_in_hbm, w_in), (w_out_hbm, w_out), (skip_hbm, skip),
            )
        )
    ]

    def load(first, second):
        pltpu.make_async_copy(first, X.at[:, own_rows], load_sem.at[0]).start()
        pltpu.make_async_copy(second, Y.at[:, own_rows], load_sem.at[1]).start()

    @pl.when(forward)
    def _():
        load(frames, cot)

    @pl.when(core == 0)
    def _():
        load(cot, frames)

    for copy in small:
        copy.start()

    pl.semaphore_wait(barrier, nt - 1 + ntile - 1)

    def send_inputs(first, second):
        remote(first, X.at[:, own_rows], in_send.at[0], in_recv.at[0], mate).start()
        edge(0)
        remote(second, Y.at[:, own_rows], in_send.at[1], in_recv.at[1], mate).start()
        edge(1)

    edge_src = pl.ds(core * (R - 1), 1)
    edge_dst = pl.ds((1 - core) * (RC + 1), 1)
    next_y = y + 2 * core - 1
    has_next = (next_y >= 0) & (next_y < ny)
    safe_y = lax.min(lax.max(next_y, 0), ny - 1)

    def edge_copies(which):
        copies = []
        for c in range(2):
            src = (frames, cot)[(c == 1) == (which == 1)]
            dst = (X, Y)[which]
            copies.append(
                remote(
                    src.at[:, edge_src], dst.at[:, edge_dst],
                    halo_send.at[which, c], halo_recv.at[which, 1 - core],
                    (tm, safe_y * 2 + c),
                )
            )
        return copies

    def edge(which):
        @pl.when(has_next)
        def _():
            for copy in edge_copies(which):
                copy.start()

    @pl.when(forward)
    def _():
        send_inputs(cot, frames)

    @pl.when(core == 0)
    def _():
        send_inputs(frames, cot)

    def edge_took(which, field):
        @pl.when(y > 0)
        def _():
            took(field.at[:, pl.ds(0, 1)], halo_recv.at[which, 0])

        @pl.when(y < ny - 1)
        def _():
            took(field.at[:, pl.ds(RC + 1, 1)], halo_recv.at[which, 1])

    small[0].wait()
    dec = jnp.exp(log_decay[...])
    whole = dec[0:1]
    for t in range(1, T):
        whole = whole * dec[t : t + 1]
    DG[tm] = jnp.broadcast_to(whole, (8, CH))
    one = jnp.ones((1, CH), F32)
    reach = None
    for i in range(T):
        a = jnp.where(forward, dec[i : i + 1], one if i == 0 else dec[T - i : T - i + 1])
        b = jnp.where(forward, 1.0 - dec[i : i + 1], one)
        c = jnp.where(forward, one, 1.0 - dec[T - 1 - i : T - i])
        reach = a if reach is None else reach * a
        COEF[i : i + 1] = a
        COEF[T + i : T + i + 1] = b
        COEF[2 * T + i : 2 * T + i + 1] = c
        COEF[3 * T + i : 3 * T + i + 1] = c * reach
    last = jnp.where(forward, one, dec[0:1])

    def weights(dst, plain, turned):
        @pl.when(forward)
        def _():
            dst[...] = plain[...]

        @pl.when(core == 0)
        def _():
            for k in range(9):
                dst[k * CH : (k + 1) * CH, :] = turned[(8 - k) * CH : (9 - k) * CH, :].T

    for copy in small[1:]:
        copy.wait()
    weights(WA, w_in, w_out)

    for d in range(1, nt):
        remote(DG.at[tm], DG.at[tm], carry_send.at[0], carry_recv.at[0], on_tm(d)).start()

    @pl.when(y == 0)
    def _():
        for field in (X, Y, S):
            field[:, 0] = jnp.zeros((T, W, CH), BF16)

    @pl.when(y == ny - 1)
    def _():
        for field in (X, Y, S):
            field[:, RC + 1] = jnp.zeros((T, W, CH), BF16)

    col = lax.broadcasted_iota(jnp.int32, (1, W, CH), 1)

    def widen(src, dst, row0, count):
        def step(k, _):
            r = row0 + k
            for t in range(T):
                v = src[t, pl.ds(r, 1)].astype(F32)
                left = jnp.where(col == 0, 0.0, pltpu.roll(v, 1, 1))
                right = jnp.where(col == W - 1, 0.0, pltpu.roll(v, W - 1, 1))
                dst[t, pl.ds(r, 1), :, 0:CH] = left.astype(BF16)
                dst[t, pl.ds(r, 1), :, CH : 2 * CH] = src[t, pl.ds(r, 1)]
                dst[t, pl.ds(r, 1), :, 2 * CH : 3 * CH] = right.astype(BF16)
            return 0

        lax.fori_loop(0, count, step, 0)

    def conv(src3, t, row0, count, weight):
        taps = jnp.concatenate(
            [src3[t, pl.ds(row0 + i, count)].reshape(count * W, 3 * CH) for i in range(3)], axis=-1
        )
        return jnp.dot(taps, weight[...], preferred_element_type=F32)

    def frame_of(i):
        return core * i + (1 - core) * (T - 1 - i)

    def local_scan(*spans):
        spans = [span for span in spans if span[1]]
        if not spans:
            return
        taps = jnp.concatenate(
            [
                jnp.concatenate([X3[:, pl.ds(row0 + i, count)] for row0, count in spans], axis=1)
                .reshape(-1, 3 * CH)
                for i in range(3)
            ],
            axis=-1,
        )
        drive = jnp.dot(taps, WA[...], preferred_element_type=F32)
        per_frame = drive.shape[0] // T
        for t in range(T):
            at = t * per_frame
            for row0, count in spans:
                rows = pl.ds(pl.multiple_of(row0 * W, W), count * W)
                DR[t, rows, :] = drive[at : at + count * W]
                at += count * W
        for row0, count in spans:
            rows = pl.ds(pl.multiple_of(row0 * W, W), count * W)
            for i in range(T):
                value = COEF[T + i : T + i + 1] * DR[frame_of(i), rows, :]
                if i:
                    value = value + COEF[i : i + 1] * LS[i - 1, rows, :]
                LS[i, rows, :] = value
            FIN[rows, :] = encode(last * value)
            send_finals(row0, count)

    def rows_of(ref, k):
        return ref.at[pl.ds(pl.multiple_of(k * W, W), W)]

    def send_finals(row0, count):
        for r in range(count):
            k = row0 + lax.rem(r + tm, count)

            @pl.when(k != tm)
            def _():
                remote(
                    rows_of(FIN, k), RF.at[tm], fin_send.at[k], carry_recv.at[1], (k, tile)
                ).start()

    took(X.at[:, pl.ds(1, R)], load_sem.at[0])
    widen(X, X3, 1 + core * R, R)
    local_scan((core * R + 1, R - 2))
    took(X.at[:, pl.ds(1, R)], in_recv.at[0])
    widen(X, X3, 1 + (1 - core) * R, R)
    if R > 2:
        local_scan(((1 - core) * (R - 1) + core, R))
    else:
        local_scan((1, RC - 2))
    edge_took(0, X)
    widen(X, X3, 0, 1)
    widen(X, X3, RC + 1, 1)
    local_scan((0, 1), (RC - 1, 1))

    others = pl.ds(0, nt - 1)
    RF[tm] = FIN[pl.ds(pl.multiple_of(tm * W, W), W), :]

    weights(WB, w_out, w_in)
    took(Y.at[:, pl.ds(1, R)], load_sem.at[1])
    took(Y.at[:, pl.ds(1, R)], in_recv.at[1])
    edge_took(1, Y)
    widen(Y, Y3, 0, RC + 2)
    for i in range(T):
        LST[i] = LS[i].T
    turned = COEF[...].T

    took(DG.at[others], carry_recv.at[0])
    took(RF.at[others], carry_recv.at[1])
    carry = jnp.zeros((W, CH), F32)
    for i in range(nt):
        k = core * i + (1 - core) * (nt - 1 - i)
        EF[k] = encode(carry)

        @pl.when(k != tm)
        def _():
            remote(EF.at[k], rows_of(INC, tm), back_send.at[k], inc_recv.at[tm], (k, tile)).start()

        if i < nt - 1:
            carry = DG[k, 0:1, :] * carry + decode(RF[k])
    INC[pl.ds(pl.multiple_of(tm * W, W), W), :] = EF[tm]

    for k in range(nt):

        @pl.when(tm != k)
        def _():
            took(rows_of(INC, k), inc_recv.at[k])

    incoming_turned = decode(INC[...].T)
    for i in range(T):
        value = (
            turned[:, 2 * T + i : 2 * T + i + 1] * LST[i]
            + turned[:, 3 * T + i : 3 * T + i + 1] * incoming_turned
        )
        ST[frame_of(i)] = value.astype(BF16)

    up = remote(
        S.at[:, pl.ds(1, 1)], S.at[:, pl.ds(RC + 1, 1)], halo_send.at[2, 0], halo_recv.at[2, 1],
        (tm, lax.max(y - 1, 0) * 2 + core),
    )
    down = remote(
        S.at[:, pl.ds(RC, 1)], S.at[:, pl.ds(0, 1)], halo_send.at[2, 1], halo_recv.at[2, 0],
        (tm, lax.min(y + 1, ny - 1) * 2 + core),
    )

    orders = (("x", "y", "z"), ("y", "z", "x"), ("z", "x", "y"))
    steps = [(da, db) for da in range(n) for db in range(n) if da or db]
    steps.sort(key=lambda s: -sum(min(d, n - d) for d in s))

    def place(g, da, db):
        a, b = orders[g][:2]
        return lax.rem(where_on[a] + da, n) * n + lax.rem(where_on[b] + db, n)

    def plane_peer(g, da, db):
        at = dict(where_on)
        for axis, d in zip(orders[g], (da, db)):
            at[axis] = lax.rem(at[axis] + d, n)
        return (at["z"] * nx + at["x"], at["y"] * 2 + core)

    for g in range(3):
        first = core * (2 - g) + (1 - core) * g
        total = jnp.zeros((CH, 3 * CH), F32)
        for t in range(T):
            other = Y3[t, pl.ds(first, RC)].reshape(pos, 3 * CH)
            total = total + jnp.dot(ST[t], other, preferred_element_type=F32)
        total = total * factor

        @pl.when(forward)
        def _():
            for j in range(3):
                block = total[:, (2 - j) * CH : (3 - j) * CH]
                G[(g * 3 + j) * CH : (g * 3 + j + 1) * CH, :] = block
                GC[(g * 3 + j) * CH : (g * 3 + j + 1) * CH, :] = encode(block)

        @pl.when(core == 0)
        def _():
            for j in range(3):
                block = total[:, j * CH : (j + 1) * CH].T
                G[(g * 3 + j) * CH : (g * 3 + j + 1) * CH, :] = block
                GC[(g * 3 + j) * CH : (g * 3 + j + 1) * CH, :] = encode(block)

        for slot, (da, db) in enumerate(steps):
            q = place(g, da, db)
            remote(
                GC.at[pl.ds(pl.multiple_of(g * group + q * chunk, chunk), chunk)],
                R1.at[g, slot], ar_send.at[0], ar_recv.at[g], plane_peer(g, da, db),
            ).start()

    def conv_out(t):
        for side, (start, stage) in enumerate(((core * R, own_out), ((1 - core) * R, MO))):
            rows = pl.ds(start + 1, R)
            direct = skip[...] * X[t, rows].reshape(R * W, CH).astype(F32)
            value = conv(S3, t, start, R, WB) + direct
            stage[t] = value.astype(BF16).reshape(R, W, CH)
        remote(MO.at[t], mate_out.at[t], mo_send.at[t], mo_recv.at[t], mate).start()

    incoming = decode(INC[...])
    for i in range(T):
        value = COEF[2 * T + i : 2 * T + i + 1] * LS[i] + COEF[3 * T + i : 3 * T + i + 1] * incoming
        S[frame_of(i), 1 : RC + 1] = value.astype(BF16).reshape(RC, W, CH)

    @pl.when(y > 0)
    def _():
        up.start()

    @pl.when(y < ny - 1)
    def _():
        down.start()

    widen(S, S3, 1, RC)

    @pl.when(y > 0)
    def _():
        took(S.at[:, pl.ds(0, 1)], halo_recv.at[2, 0])

    @pl.when(y < ny - 1)
    def _():
        took(S.at[:, pl.ds(0, 1)], halo_recv.at[2, 1])

    widen(S, S3, 0, 1)
    widen(S, S3, RC + 1, 1)

    conv_out(0)
    conv_out(1)
    for g in range(3):
        took(R1.at[g], ar_recv.at[g])
        value = G[pl.ds(pl.multiple_of(g * group + place(g, 0, 0) * chunk, chunk), chunk), :]
        for slot in range(n * n - 1):
            value = value + decode(R1[g, slot])
        c = orders[g][2]
        r = where_on[c]
        R3[g, r] = value
        for d in range(1, n):
            remote(
                R3.at[g, r], R3.at[g, r], ar_send.at[1], ar_recv.at[3 + g], axis_peer(c, d)
            ).start()
    conv_out(2)
    base = core * half
    for g in range(3):
        took(R3.at[g, pl.ds(0, n - 1)], ar_recv.at[3 + g])
        value = R3[g, 0]
        for k in range(1, n):
            value = value + R3[g, k]
        rows = pl.ds(pl.multiple_of(base + g * group + place(g, 0, 0) * chunk, chunk), chunk)
        sums[rows, :] = value.astype(BF16)
        for da, db in steps:
            remote(
                sums.at[rows], sums.at[rows], ar_send.at[2], ar_recv.at[6 + g],
                plane_peer(g, da, db),
            ).start()
    conv_out(3)
    to_mate = []
    for g in range(3):
        rows = pl.ds(pl.multiple_of(base + g * group, group), group)
        took(sums.at[pl.ds(0, group - chunk)], ar_recv.at[6 + g])
        to_mate.append(
            remote(sums.at[rows], sums.at[rows], ar_send.at[3 + g], ar_recv.at[9 + g], mate)
        )
        to_mate[-1].start()

    for t in range(T):
        took(MO.at[t], mo_recv.at[t])
    for copy in to_mate:
        copy.wait_recv()

    for copy in to_mate:
        copy.wait_send()
    for t in range(T):
        took(MO.at[t], mo_send.at[t])
    took(R1, ar_send.at[0])
    took(R3.at[:, pl.ds(0, n - 1)], ar_send.at[1])
    took(sums.at[pl.ds(0, half - 3 * chunk)], ar_send.at[2])
    took(DG.at[others], carry_send.at[0])
    for k in range(nt):

        @pl.when(tm != k)
        def _():
            took(EF.at[0], fin_send.at[k])
            took(EF.at[0], back_send.at[k])

    for k in range(2):
        took(X.at[:, pl.ds(1, R)], in_send.at[k])

    @pl.when(has_next)
    def _():
        for which in range(2):
            for copy in edge_copies(which):
                copy.wait_send()

    @pl.when(y > 0)
    def _():
        up.wait_send()

    @pl.when(y < ny - 1)
    def _():
        down.wait_send()


def store_kernel(own_out, mate_out, sums, output, grad_frames, grad_in, grad_out, wide, sem):
    forward = lax.rem(lax.axis_index("tile"), 2) == 1
    half = grad_in.shape[0]

    def put(first, second):
        pltpu.make_async_copy(own_out, first, sem.at[0]).start()
        pltpu.make_async_copy(mate_out, second, sem.at[1]).start()

    @pl.when(forward)
    def _():
        put(output, grad_frames)

    @pl.when(jnp.logical_not(forward))
    def _():
        put(grad_frames, output)

    copies = []
    for k, dst in enumerate((grad_in, grad_out)):
        wide[k] = sums[k * half : (k + 1) * half, :].astype(F32)
        copies.append(pltpu.make_async_copy(wide.at[k], dst, sem.at[2 + k]))
        copies[-1].start()
    pltpu.make_async_copy(own_out, output, sem.at[0]).wait()
    pltpu.make_async_copy(mate_out, grad_frames, sem.at[1]).wait()
    for copy in copies:
        copy.wait()


def solution(mesh):
    nt, ntile = mesh.shape["tm"], mesh.shape["tile"]
    nx = math.isqrt(nt)
    ny = ntile // 2

    def step(frames, cot, w_in, w_out, skip, log_decay):
        T, R, W, CH = frames.shape
        factor = 1.0 / math.sqrt(T * nt * R * ntile * W)
        RC = 2 * R
        pos = RC * W
        n = nx
        half = 9 * CH
        chunk = half // 3 // (n * n)
        vm = pltpu.VMEM
        field = vm((T, RC + 2, W, CH), BF16)
        field3 = vm((T, RC + 2, W, 3 * CH), BF16)
        dma = pltpu.SemaphoreType.DMA
        hbm = pl.BlockSpec(memory_space=pl.ANY)
        vmem = pl.BlockSpec(memory_space=pltpu.VMEM)
        own_out, mate_out, sums = pl.pallas_call(
            functools.partial(chain_kernel, (nt, nx, ny, factor)),
            out_shape=(
                vm(frames.shape, BF16),
                vm(frames.shape, BF16),
                vm((2 * half, CH), BF16),
            ),
            in_specs=[hbm] * 6,
            out_specs=[vmem] * 3,
            scratch_shapes=[
                field, field, field, field3, field3, field3, vm((T, CH, pos), BF16),
                vm((half, CH), BF16), vm((half, CH), BF16), vm((1, CH), F32), vm((T, CH), F32),
                vm((half, CH), BF16), vm((half, CH), BF16), vm((4 * T, CH), F32), vm((nt, 8, CH), F32),
                vm((T, pos, CH), F32), vm((T, pos, CH), F32), vm((T, CH, pos), F32), vm((pos, CH), BF16),
                vm((nt, W, CH), BF16), vm((nt, W, CH), BF16), vm((pos, CH), BF16),
                vm((half, CH), F32), vm((half, CH), BF16),
                vm((3, n * n - 1, chunk, CH), BF16), vm((3, n, chunk, CH), F32), vm(frames.shape, BF16),
                dma((6,)), dma((2,)), dma((2,)), dma((3, 2)), dma((3, 2)),
                dma((1,)), dma((2,)), dma((nt,)), dma((nt,)), dma((nt,)),
                dma((6,)), dma((12,)), dma((T,)), dma((T,)),
            ],
            compiler_params=pltpu.CompilerParams(
                collective_id=0, has_side_effects=True, vmem_limit_bytes=65_300_000
            ),
        )(
            frames, cot, w_in.reshape(half, CH), w_out.reshape(half, CH),
            skip.reshape(1, CH), log_decay,
        )
        res = pl.pallas_call(
            store_kernel,
            out_shape=(
                jax.ShapeDtypeStruct(frames.shape, BF16),
                jax.ShapeDtypeStruct(frames.shape, BF16),
                jax.ShapeDtypeStruct((half, CH), F32),
                jax.ShapeDtypeStruct((half, CH), F32),
            ),
            in_specs=[vmem] * 3,
            out_specs=[hbm] * 4,
            scratch_shapes=[vm((2, half, CH), F32), dma((4,))],
            compiler_params=pltpu.CompilerParams(vmem_limit_bytes=8 * 2**20),
        )(own_out, mate_out, sums)
        return (res[0], res[1], res[2].reshape(3, 3, CH, CH), res[3].reshape(3, 3, CH, CH))

    block = P("tm", "tile", None, None)
    return jax.shard_map(
        step,
        mesh=mesh,
        in_specs=(block, block, P(), P(), P(), P("tm", None)),
        out_specs=(block, block, P(), P()),
        check_vma=False,
    )
```

```python
import functools
import math

import jax
import jax.numpy as jnp
from jax import lax
from jax.experimental import pallas as pl
from jax.experimental.pallas import tpu as pltpu
from jax.sharding import PartitionSpec as P

MESH = pl.DeviceIdType.MESH
F32 = jnp.float32
BF16 = jnp.bfloat16
ROOT = 5


def encode(v):
    square = v * v
    return (v * (square * square)).astype(BF16)


def decode(code):
    w = code.astype(F32)
    root = jnp.exp2(jnp.log2(jnp.abs(w)) * (1.0 / ROOT))
    return jnp.where(w < 0.0, -root, root)


def chain_kernel(
    dims,
    frames, cot, w_in_hbm, w_out_hbm, skip_hbm, log_decay_hbm,
    own_out, mate_out, sums,
    X, Y, S, X3, Y3, S3, ST,
    w_in, w_out, skip, log_decay, WA, WB, COEF, DG,
    DR, LS, FIN, RF, EF, INC,
    G, GC, R1, R3, MO,
    load_sem, in_send, in_recv, halo_send, halo_recv,
    carry_send, carry_recv, fin_send, back_send, inc_recv, ar_send, ar_recv, mo_send, mo_recv,
):
    nt, nx, ny, factor = dims
    T, R, W, CH = frames.shape
    RC = 2 * R
    n = nx
    pos = RC * W
    half = 9 * CH
    group = half // 3
    chunk = group // (n * n)

    tm = lax.axis_index("tm")
    tile = lax.axis_index("tile")
    ntile = ny * 2
    z, x = lax.div(tm, nx), lax.rem(tm, nx)
    y, core = lax.div(tile, 2), lax.rem(tile, 2)
    forward = core == 1
    mate = (tm, y * 2 + 1 - core)

    def on_tm(d):
        return (lax.rem(tm + d, nt), tile)

    where_on = {"x": x, "y": y, "z": z}

    def axis_peer(axis, d):
        if axis == "x":
            return (z * nx + lax.rem(x + d, nx), tile)
        if axis == "z":
            return (lax.rem(z + d, nt // nx) * nx + x, tile)
        return (tm, lax.rem(y + d, ny) * 2 + core)

    def remote(src, dst, send, recv, device):
        return pltpu.make_async_remote_copy(
            src, dst, send, recv, device_id=device, device_id_type=MESH
        )

    def took(ref, sem):
        pltpu.make_async_copy(ref, ref, sem).wait()

    barrier = pltpu.get_barrier_semaphore()
    for d in range(1, nt):
        pl.semaphore_signal(barrier, inc=1, device_id=on_tm(d), device_id_type=MESH)
    for d in range(1, ntile):
        pl.semaphore_signal(
            barrier, inc=1, device_id=(tm, lax.rem(tile + d, ntile)), device_id_type=MESH
        )

    own_rows = pl.ds(1 + core * R, R)
    small = [
        pltpu.make_async_copy(src, dst, load_sem.at[2 + k])
        for k, (src, dst) in enumerate(
            (
                (log_decay_hbm, log_decay), (w_in_hbm, w_in), (w_out_hbm, w_out), (skip_hbm, skip),
            )
        )
    ]

    def load(first, second):
        pltpu.make_async_copy(first, X.at[:, own_rows], load_sem.at[0]).start()
        pltpu.make_async_copy(second, Y.at[:, own_rows], load_sem.at[1]).start()

    @pl.when(forward)
    def _():
        load(frames, cot)

    @pl.when(core == 0)
    def _():
        load(cot, frames)

    for copy in small:
        copy.start()

    pl.semaphore_wait(barrier, nt - 1 + ntile - 1)

    def send_inputs(first, second):
        remote(first, X.at[:, own_rows], in_send.at[0], in_recv.at[0], mate).start()
        edge(0)
        remote(second, Y.at[:, own_rows], in_send.at[1], in_recv.at[1], mate).start()
        edge(1)

    edge_src = pl.ds(core * (R - 1), 1)
    edge_dst = pl.ds((1 - core) * (RC + 1), 1)
    next_y = y + 2 * core - 1
    has_next = (next_y >= 0) & (next_y < ny)
    safe_y = lax.min(lax.max(next_y, 0), ny - 1)

    def edge_copies(which):
        copies = []
        for c in range(2):
            src = (frames, cot)[(c == 1) == (which == 1)]
            dst = (X, Y)[which]
            copies.append(
                remote(
                    src.at[:, edge_src], dst.at[:, edge_dst],
                    halo_send.at[which, c], halo_recv.at[which, 1 - core],
                    (tm, safe_y * 2 + c),
                )
            )
        return copies

    def edge(which):
        @pl.when(has_next)
        def _():
            for copy in edge_copies(which):
                copy.start()

    @pl.when(forward)
    def _():
        send_inputs(cot, frames)

    @pl.when(core == 0)
    def _():
        send_inputs(frames, cot)

    def edge_took(which, field):
        @pl.when(y > 0)
        def _():
            took(field.at[:, pl.ds(0, 1)], halo_recv.at[which, 0])

        @pl.when(y < ny - 1)
        def _():
            took(field.at[:, pl.ds(RC + 1, 1)], halo_recv.at[which, 1])

    small[0].wait()
    dec = jnp.exp(log_decay[...])
    whole = dec[0:1]
    for t in range(1, T):
        whole = whole * dec[t : t + 1]
    DG[tm] = jnp.broadcast_to(whole, (8, CH))
    one = jnp.ones((1, CH), F32)
    reach = None
    for i in range(T):
        a = jnp.where(forward, dec[i : i + 1], one if i == 0 else dec[T - i : T - i + 1])
        b = jnp.where(forward, 1.0 - dec[i : i + 1], one)
        c = jnp.where(forward, one, 1.0 - dec[T - 1 - i : T - i])
        reach = a if reach is None else reach * a
        COEF[i : i + 1] = a
        COEF[T + i : T + i + 1] = b
        COEF[2 * T + i : 2 * T + i + 1] = c
        COEF[3 * T + i : 3 * T + i + 1] = c * reach
    last = jnp.where(forward, one, dec[0:1])

    def weights(dst, plain, turned):
        @pl.when(forward)
        def _():
            dst[...] = plain[...]

        @pl.when(core == 0)
        def _():
            for k in range(9):
                dst[k * CH : (k + 1) * CH, :] = turned[(8 - k) * CH : (9 - k) * CH, :].T

    for copy in small[1:]:
        copy.wait()
    weights(WA, w_in, w_out)

    for d in range(1, nt):
        remote(DG.at[tm], DG.at[tm], carry_send.at[0], carry_recv.at[0], on_tm(d)).start()

    @pl.when(y == 0)
    def _():
        for field in (X, Y, S):
            field[:, 0] = jnp.zeros((T, W, CH), BF16)

    @pl.when(y == ny - 1)
    def _():
        for field in (X, Y, S):
            field[:, RC + 1] = jnp.zeros((T, W, CH), BF16)

    col = lax.broadcasted_iota(jnp.int32, (1, W, CH), 1)

    def widen(src, dst, row0, count):
        def step(k, _):
            r = row0 + k
            for t in range(T):
                v = src[t, pl.ds(r, 1)].astype(F32)
                left = jnp.where(col == 0, 0.0, pltpu.roll(v, 1, 1))
                right = jnp.where(col == W - 1, 0.0, pltpu.roll(v, W - 1, 1))
                dst[t, pl.ds(r, 1), :, 0:CH] = left.astype(BF16)
                dst[t, pl.ds(r, 1), :, CH : 2 * CH] = src[t, pl.ds(r, 1)]
                dst[t, pl.ds(r, 1), :, 2 * CH : 3 * CH] = right.astype(BF16)
            return 0

        lax.fori_loop(0, count, step, 0)

    def conv(src3, t, row0, count, weight):
        taps = jnp.concatenate(
            [src3[t, pl.ds(row0 + i, count)].reshape(count * W, 3 * CH) for i in range(3)], axis=-1
        )
        return jnp.dot(taps, weight[...], preferred_element_type=F32)

    def frame_of(i):
        return core * i + (1 - core) * (T - 1 - i)

    def local_scan(*spans):
        spans = [span for span in spans if span[1]]
        if not spans:
            return
        taps = jnp.concatenate(
            [
                jnp.concatenate([X3[:, pl.ds(row0 + i, count)] for row0, count in spans], axis=1)
                .reshape(-1, 3 * CH)
                for i in range(3)
            ],
            axis=-1,
        )
        drive = jnp.dot(taps, WA[...], preferred_element_type=F32)
        per_frame = drive.shape[0] // T
        for t in range(T):
            at = t * per_frame
            for row0, count in spans:
                rows = pl.ds(pl.multiple_of(row0 * W, W), count * W)
                DR[t, rows, :] = drive[at : at + count * W]
                at += count * W
        for row0, count in spans:
            rows = pl.ds(pl.multiple_of(row0 * W, W), count * W)
            for i in range(T):
                value = COEF[T + i : T + i + 1] * DR[frame_of(i), rows, :]
                if i:
                    value = value + COEF[i : i + 1] * LS[i - 1, rows, :]
                LS[i, rows, :] = value
            FIN[rows, :] = encode(last * value)
            send_finals(row0, count)

    def rows_of(ref, k):
        return ref.at[pl.ds(pl.multiple_of(k * W, W), W)]

    def send_finals(row0, count):
        for r in range(count):
            k = row0 + lax.rem(r + tm, count)

            @pl.when(k != tm)
            def _():
                remote(
                    rows_of(FIN, k), RF.at[tm], fin_send.at[k], carry_recv.at[1], (k, tile)
                ).start()

    took(X.at[:, pl.ds(1, R)], load_sem.at[0])
    widen(X, X3, 1 + core * R, R)
    local_scan((core * R + 1, R - 2))
    took(X.at[:, pl.ds(1, R)], in_recv.at[0])
    widen(X, X3, 1 + (1 - core) * R, R)
    if R > 2:
        local_scan(((1 - core) * (R - 1) + core, R))
    else:
        local_scan((1, RC - 2))
    edge_took(0, X)
    widen(X, X3, 0, 1)
    widen(X, X3, RC + 1, 1)
    local_scan((0, 1), (RC - 1, 1))

    others = pl.ds(0, nt - 1)
    RF[tm] = FIN[pl.ds(pl.multiple_of(tm * W, W), W), :]

    weights(WB, w_out, w_in)
    took(Y.at[:, pl.ds(1, R)], load_sem.at[1])
    took(Y.at[:, pl.ds(1, R)], in_recv.at[1])
    edge_took(1, Y)
    widen(Y, Y3, 0, RC + 2)

    took(DG.at[others], carry_recv.at[0])
    took(RF.at[others], carry_recv.at[1])
    carry = jnp.zeros((W, CH), F32)
    for i in range(nt):
        k = core * i + (1 - core) * (nt - 1 - i)
        EF[k] = encode(carry)

        @pl.when(k != tm)
        def _():
            remote(EF.at[k], rows_of(INC, tm), back_send.at[k], inc_recv.at[tm], (k, tile)).start()

        if i < nt - 1:
            carry = DG[k, 0:1, :] * carry + decode(RF[k])
    INC[pl.ds(pl.multiple_of(tm * W, W), W), :] = EF[tm]

    def finish(row0, count):
        for k in range(row0, row0 + count):

            @pl.when(tm != k)
            def _():
                took(rows_of(INC, k), inc_recv.at[k])

        rows = slice(row0 * W, (row0 + count) * W)
        incoming = decode(INC[rows, :])
        for i in range(T):
            value = (
                COEF[2 * T + i : 2 * T + i + 1] * LS[i, rows, :]
                + COEF[3 * T + i : 3 * T + i + 1] * incoming
            )
            S[frame_of(i), 1 + row0 : 1 + row0 + count] = value.astype(BF16).reshape(count, W, CH)

    finish(1, RC - 2)
    finish(0, 1)
    finish(RC - 1, 1)

    up = remote(
        S.at[:, pl.ds(1, 1)], S.at[:, pl.ds(RC + 1, 1)], halo_send.at[2, 0], halo_recv.at[2, 1],
        (tm, lax.max(y - 1, 0) * 2 + core),
    )
    down = remote(
        S.at[:, pl.ds(RC, 1)], S.at[:, pl.ds(0, 1)], halo_send.at[2, 1], halo_recv.at[2, 0],
        (tm, lax.min(y + 1, ny - 1) * 2 + core),
    )

    @pl.when(y > 0)
    def _():
        up.start()

    @pl.when(y < ny - 1)
    def _():
        down.start()

    orders = (("x", "y", "z"), ("y", "z", "x"), ("z", "x", "y"))
    steps = [(da, db) for da in range(n) for db in range(n) if da or db]
    steps.sort(key=lambda s: -sum(min(d, n - d) for d in s))

    def place(g, da, db):
        a, b = orders[g][:2]
        return lax.rem(where_on[a] + da, n) * n + lax.rem(where_on[b] + db, n)

    def plane_peer(g, da, db):
        at = dict(where_on)
        for axis, d in zip(orders[g], (da, db)):
            at[axis] = lax.rem(at[axis] + d, n)
        return (at["z"] * nx + at["x"], at["y"] * 2 + core)

    for t in range(T):
        ST[t] = S[t, 1 : RC + 1].reshape(pos, CH).T
    for g in range(3):
        first = core * (2 - g) + (1 - core) * g
        total = jnp.zeros((CH, 3 * CH), F32)
        for t in range(T):
            other = Y3[t, pl.ds(first, RC)].reshape(pos, 3 * CH)
            total = total + jnp.dot(ST[t], other, preferred_element_type=F32)
        total = total * factor

        @pl.when(forward)
        def _():
            for j in range(3):
                block = total[:, (2 - j) * CH : (3 - j) * CH]
                G[(g * 3 + j) * CH : (g * 3 + j + 1) * CH, :] = block
                GC[(g * 3 + j) * CH : (g * 3 + j + 1) * CH, :] = encode(block)

        @pl.when(core == 0)
        def _():
            for j in range(3):
                block = total[:, j * CH : (j + 1) * CH].T
                G[(g * 3 + j) * CH : (g * 3 + j + 1) * CH, :] = block
                GC[(g * 3 + j) * CH : (g * 3 + j + 1) * CH, :] = encode(block)

        for slot, (da, db) in enumerate(steps):
            q = place(g, da, db)
            remote(
                GC.at[pl.ds(pl.multiple_of(g * group + q * chunk, chunk), chunk)],
                R1.at[g, slot], ar_send.at[0], ar_recv.at[g], plane_peer(g, da, db),
            ).start()

    def conv_out(t):
        for side, (start, stage) in enumerate(((core * R, own_out), ((1 - core) * R, MO))):
            rows = pl.ds(start + 1, R)
            direct = skip[...] * X[t, rows].reshape(R * W, CH).astype(F32)
            value = conv(S3, t, start, R, WB) + direct
            stage[t] = value.astype(BF16).reshape(R, W, CH)
        remote(MO.at[t], mate_out.at[t], mo_send.at[t], mo_recv.at[t], mate).start()

    widen(S, S3, 1, RC)

    @pl.when(y > 0)
    def _():
        took(S.at[:, pl.ds(0, 1)], halo_recv.at[2, 0])

    @pl.when(y < ny - 1)
    def _():
        took(S.at[:, pl.ds(0, 1)], halo_recv.at[2, 1])

    widen(S, S3, 0, 1)
    widen(S, S3, RC + 1, 1)

    conv_out(0)
    conv_out(1)
    for g in range(3):
        took(R1.at[g], ar_recv.at[g])
        value = G[pl.ds(pl.multiple_of(g * group + place(g, 0, 0) * chunk, chunk), chunk), :]
        for slot in range(n * n - 1):
            value = value + decode(R1[g, slot])
        c = orders[g][2]
        r = where_on[c]
        R3[g, r] = value
        for d in range(1, n):
            remote(
                R3.at[g, r], R3.at[g, r], ar_send.at[1], ar_recv.at[3 + g], axis_peer(c, d)
            ).start()
    conv_out(2)
    base = core * half
    for g in range(3):
        took(R3.at[g, pl.ds(0, n - 1)], ar_recv.at[3 + g])
        value = R3[g, 0]
        for k in range(1, n):
            value = value + R3[g, k]
        rows = pl.ds(pl.multiple_of(base + g * group + place(g, 0, 0) * chunk, chunk), chunk)
        sums[rows, :] = value.astype(BF16)
        for da, db in steps:
            remote(
                sums.at[rows], sums.at[rows], ar_send.at[2], ar_recv.at[6 + g],
                plane_peer(g, da, db),
            ).start()
    conv_out(3)
    to_mate = []
    for g in range(3):
        rows = pl.ds(pl.multiple_of(base + g * group, group), group)
        took(sums.at[pl.ds(0, group - chunk)], ar_recv.at[6 + g])
        to_mate.append(
            remote(sums.at[rows], sums.at[rows], ar_send.at[3 + g], ar_recv.at[9 + g], mate)
        )
        to_mate[-1].start()

    for t in range(T):
        took(MO.at[t], mo_recv.at[t])
    for copy in to_mate:
        copy.wait_recv()

    for copy in to_mate:
        copy.wait_send()
    for t in range(T):
        took(MO.at[t], mo_send.at[t])
    took(R1, ar_send.at[0])
    took(R3.at[:, pl.ds(0, n - 1)], ar_send.at[1])
    took(sums.at[pl.ds(0, half - 3 * chunk)], ar_send.at[2])
    took(DG.at[others], carry_send.at[0])
    for k in range(nt):

        @pl.when(tm != k)
        def _():
            took(EF.at[0], fin_send.at[k])
            took(EF.at[0], back_send.at[k])

    for k in range(2):
        took(X.at[:, pl.ds(1, R)], in_send.at[k])

    @pl.when(has_next)
    def _():
        for which in range(2):
            for copy in edge_copies(which):
                copy.wait_send()

    @pl.when(y > 0)
    def _():
        up.wait_send()

    @pl.when(y < ny - 1)
    def _():
        down.wait_send()


def store_kernel(own_out, mate_out, sums, output, grad_frames, grad_in, grad_out, wide, sem):
    forward = lax.rem(lax.axis_index("tile"), 2) == 1
    half = grad_in.shape[0]

    def put(first, second):
        pltpu.make_async_copy(own_out, first, sem.at[0]).start()
        pltpu.make_async_copy(mate_out, second, sem.at[1]).start()

    @pl.when(forward)
    def _():
        put(output, grad_frames)

    @pl.when(jnp.logical_not(forward))
    def _():
        put(grad_frames, output)

    copies = []
    for k, dst in enumerate((grad_in, grad_out)):
        wide[k] = sums[k * half : (k + 1) * half, :].astype(F32)
        copies.append(pltpu.make_async_copy(wide.at[k], dst, sem.at[2 + k]))
        copies[-1].start()
    pltpu.make_async_copy(own_out, output, sem.at[0]).wait()
    pltpu.make_async_copy(mate_out, grad_frames, sem.at[1]).wait()
    for copy in copies:
        copy.wait()


def solution(mesh):
    nt, ntile = mesh.shape["tm"], mesh.shape["tile"]
    nx = math.isqrt(nt)
    ny = ntile // 2

    def step(frames, cot, w_in, w_out, skip, log_decay):
        T, R, W, CH = frames.shape
        factor = 1.0 / math.sqrt(T * nt * R * ntile * W)
        RC = 2 * R
        pos = RC * W
        n = nx
        half = 9 * CH
        chunk = half // 3 // (n * n)
        vm = pltpu.VMEM
        field = vm((T, RC + 2, W, CH), BF16)
        field3 = vm((T, RC + 2, W, 3 * CH), BF16)
        dma = pltpu.SemaphoreType.DMA
        hbm = pl.BlockSpec(memory_space=pl.ANY)
        vmem = pl.BlockSpec(memory_space=pltpu.VMEM)
        own_out, mate_out, sums = pl.pallas_call(
            functools.partial(chain_kernel, (nt, nx, ny, factor)),
            out_shape=(
                vm(frames.shape, BF16),
                vm(frames.shape, BF16),
                vm((2 * half, CH), BF16),
            ),
            in_specs=[hbm] * 6,
            out_specs=[vmem] * 3,
            scratch_shapes=[
                field, field, field, field3, field3, field3, vm((T, CH, pos), BF16),
                vm((half, CH), BF16), vm((half, CH), BF16), vm((1, CH), F32), vm((T, CH), F32),
                vm((half, CH), BF16), vm((half, CH), BF16), vm((4 * T, CH), F32), vm((nt, 8, CH), F32),
                vm((T, pos, CH), F32), vm((T, pos, CH), F32), vm((pos, CH), BF16),
                vm((nt, W, CH), BF16), vm((nt, W, CH), BF16), vm((pos, CH), BF16),
                vm((half, CH), F32), vm((half, CH), BF16),
                vm((3, n * n - 1, chunk, CH), BF16), vm((3, n, chunk, CH), F32), vm(frames.shape, BF16),
                dma((6,)), dma((2,)), dma((2,)), dma((3, 2)), dma((3, 2)),
                dma((1,)), dma((2,)), dma((nt,)), dma((nt,)), dma((nt,)),
                dma((6,)), dma((12,)), dma((T,)), dma((T,)),
            ],
            compiler_params=pltpu.CompilerParams(
                collective_id=0, has_side_effects=True, vmem_limit_bytes=65_300_000
            ),
        )(
            frames, cot, w_in.reshape(half, CH), w_out.reshape(half, CH),
            skip.reshape(1, CH), log_decay,
        )
        res = pl.pallas_call(
            store_kernel,
            out_shape=(
                jax.ShapeDtypeStruct(frames.shape, BF16),
                jax.ShapeDtypeStruct(frames.shape, BF16),
                jax.ShapeDtypeStruct((half, CH), F32),
                jax.ShapeDtypeStruct((half, CH), F32),
            ),
            in_specs=[vmem] * 3,
            out_specs=[hbm] * 4,
            scratch_shapes=[vm((2, half, CH), F32), dma((4,))],
            compiler_params=pltpu.CompilerParams(vmem_limit_bytes=8 * 2**20),
        )(own_out, mate_out, sums)
        return (res[0], res[1], res[2].reshape(3, 3, CH, CH), res[3].reshape(3, 3, CH, CH))

    block = P("tm", "tile", None, None)
    return jax.shard_map(
        step,
        mesh=mesh,
        in_specs=(block, block, P(), P(), P(), P("tm", None)),
        out_specs=(block, block, P(), P()),
        check_vma=False,
    )
```

```python
import functools
import math

import jax
import jax.numpy as jnp
from jax import lax
from jax.experimental import pallas as pl
from jax.experimental.pallas import tpu as pltpu
from jax.sharding import PartitionSpec as P

MESH = pl.DeviceIdType.MESH
F32 = jnp.float32
BF16 = jnp.bfloat16
ROOT = 5


def encode(v):
    square = v * v
    return (v * (square * square)).astype(BF16)


def decode(code):
    w = code.astype(F32)
    root = jnp.exp2(jnp.log2(jnp.abs(w)) * (1.0 / ROOT))
    return jnp.where(w < 0.0, -root, root)


def chain_kernel(
    dims,
    frames, cot, w_in_hbm, w_out_hbm, skip_hbm, log_decay_hbm,
    own_out, mate_out, sums,
    X, Y, S, X3, Y3, S3, ST,
    w_in, w_out, skip, log_decay, WA, WB, COEF, DG,
    DR, LS, FIN, RF, EF, INC,
    G, GC, R1, R3, MO,
    load_sem, in_send, in_recv, halo_send, halo_recv,
    carry_send, carry_recv, fin_send, back_send, inc_recv, ar_send, ar_recv, mo_send, mo_recv,
):
    nt, nx, ny, factor = dims
    T, R, W, CH = frames.shape
    RC = 2 * R
    n = nx
    pos = RC * W
    half = 9 * CH
    group = half // 3
    chunk = group // (n * n)

    tm = lax.axis_index("tm")
    tile = lax.axis_index("tile")
    ntile = ny * 2
    z, x = lax.div(tm, nx), lax.rem(tm, nx)
    y, core = lax.div(tile, 2), lax.rem(tile, 2)
    forward = core == 1
    mate = (tm, y * 2 + 1 - core)

    def on_tm(d):
        return (lax.rem(tm + d, nt), tile)

    where_on = {"x": x, "y": y, "z": z}

    def axis_peer(axis, d):
        if axis == "x":
            return (z * nx + lax.rem(x + d, nx), tile)
        if axis == "z":
            return (lax.rem(z + d, nt // nx) * nx + x, tile)
        return (tm, lax.rem(y + d, ny) * 2 + core)

    def remote(src, dst, send, recv, device):
        return pltpu.make_async_remote_copy(
            src, dst, send, recv, device_id=device, device_id_type=MESH
        )

    def took(ref, sem):
        pltpu.make_async_copy(ref, ref, sem).wait()

    barrier = pltpu.get_barrier_semaphore()
    for d in range(1, nt):
        pl.semaphore_signal(barrier, inc=1, device_id=on_tm(d), device_id_type=MESH)
    for d in range(1, ntile):
        pl.semaphore_signal(
            barrier, inc=1, device_id=(tm, lax.rem(tile + d, ntile)), device_id_type=MESH
        )

    own_rows = pl.ds(1 + core * R, R)
    small = [
        pltpu.make_async_copy(src, dst, load_sem.at[2 + k])
        for k, (src, dst) in enumerate(
            (
                (log_decay_hbm, log_decay), (w_in_hbm, w_in), (w_out_hbm, w_out), (skip_hbm, skip),
            )
        )
    ]

    def load(first, second):
        pltpu.make_async_copy(first, X.at[:, own_rows], load_sem.at[0]).start()
        pltpu.make_async_copy(second, Y.at[:, own_rows], load_sem.at[1]).start()

    @pl.when(forward)
    def _():
        load(frames, cot)

    @pl.when(core == 0)
    def _():
        load(cot, frames)

    for copy in small:
        copy.start()

    pl.semaphore_wait(barrier, nt - 1 + ntile - 1)

    def send_inputs(first, second):
        remote(first, X.at[:, own_rows], in_send.at[0], in_recv.at[0], mate).start()
        edge(0)
        remote(second, Y.at[:, own_rows], in_send.at[1], in_recv.at[1], mate).start()
        edge(1)

    edge_src = pl.ds(core * (R - 1), 1)
    edge_dst = pl.ds((1 - core) * (RC + 1), 1)
    next_y = y + 2 * core - 1
    has_next = (next_y >= 0) & (next_y < ny)
    safe_y = lax.min(lax.max(next_y, 0), ny - 1)

    def edge_copies(which):
        copies = []
        for c in range(2):
            src = (frames, cot)[(c == 1) == (which == 1)]
            dst = (X, Y)[which]
            copies.append(
                remote(
                    src.at[:, edge_src], dst.at[:, edge_dst],
                    halo_send.at[which, c], halo_recv.at[which, 1 - core],
                    (tm, safe_y * 2 + c),
                )
            )
        return copies

    def edge(which):
        @pl.when(has_next)
        def _():
            for copy in edge_copies(which):
                copy.start()

    @pl.when(forward)
    def _():
        send_inputs(cot, frames)

    @pl.when(core == 0)
    def _():
        send_inputs(frames, cot)

    def edge_took(which, field):
        @pl.when(y > 0)
        def _():
            took(field.at[:, pl.ds(0, 1)], halo_recv.at[which, 0])

        @pl.when(y < ny - 1)
        def _():
            took(field.at[:, pl.ds(RC + 1, 1)], halo_recv.at[which, 1])

    small[0].wait()
    dec = jnp.exp(log_decay[...])
    whole = dec[0:1]
    for t in range(1, T):
        whole = whole * dec[t : t + 1]
    DG[tm] = jnp.broadcast_to(whole, (8, CH))
    one = jnp.ones((1, CH), F32)
    reach = None
    for i in range(T):
        a = jnp.where(forward, dec[i : i + 1], one if i == 0 else dec[T - i : T - i + 1])
        b = jnp.where(forward, 1.0 - dec[i : i + 1], one)
        c = jnp.where(forward, one, 1.0 - dec[T - 1 - i : T - i])
        reach = a if reach is None else reach * a
        COEF[i : i + 1] = a
        COEF[T + i : T + i + 1] = b
        COEF[2 * T + i : 2 * T + i + 1] = c
        COEF[3 * T + i : 3 * T + i + 1] = c * reach
    last = jnp.where(forward, one, dec[0:1])

    def weights(dst, plain, turned):
        @pl.when(forward)
        def _():
            dst[...] = plain[...]

        @pl.when(core == 0)
        def _():
            for k in range(9):
                dst[k * CH : (k + 1) * CH, :] = turned[(8 - k) * CH : (9 - k) * CH, :].T

    for copy in small[1:]:
        copy.wait()
    weights(WA, w_in, w_out)

    for d in range(1, nt):
        remote(DG.at[tm], DG.at[tm], carry_send.at[0], carry_recv.at[0], on_tm(d)).start()

    @pl.when(y == 0)
    def _():
        for field in (X, Y, S):
            field[:, 0] = jnp.zeros((T, W, CH), BF16)

    @pl.when(y == ny - 1)
    def _():
        for field in (X, Y, S):
            field[:, RC + 1] = jnp.zeros((T, W, CH), BF16)

    col = lax.broadcasted_iota(jnp.int32, (1, W, CH), 1)

    def widen(src, dst, row0, count):
        def step(k, _):
            r = row0 + k
            for t in range(T):
                v = src[t, pl.ds(r, 1)].astype(F32)
                left = jnp.where(col == 0, 0.0, pltpu.roll(v, 1, 1))
                right = jnp.where(col == W - 1, 0.0, pltpu.roll(v, W - 1, 1))
                dst[t, pl.ds(r, 1), :, 0:CH] = left.astype(BF16)
                dst[t, pl.ds(r, 1), :, CH : 2 * CH] = src[t, pl.ds(r, 1)]
                dst[t, pl.ds(r, 1), :, 2 * CH : 3 * CH] = right.astype(BF16)
            return 0

        lax.fori_loop(0, count, step, 0)

    def conv(src3, t, row0, count, weight):
        taps = jnp.concatenate(
            [src3[t, pl.ds(row0 + i, count)].reshape(count * W, 3 * CH) for i in range(3)], axis=-1
        )
        return jnp.dot(taps, weight[...], preferred_element_type=F32)

    def frame_of(i):
        return core * i + (1 - core) * (T - 1 - i)

    def local_scan(*spans):
        spans = [span for span in spans if span[1]]
        if not spans:
            return
        taps = jnp.concatenate(
            [
                jnp.concatenate([X3[:, pl.ds(row0 + i, count)] for row0, count in spans], axis=1)
                .reshape(-1, 3 * CH)
                for i in range(3)
            ],
            axis=-1,
        )
        drive = jnp.dot(taps, WA[...], preferred_element_type=F32)
        per_frame = drive.shape[0] // T
        for t in range(T):
            at = t * per_frame
            for row0, count in spans:
                rows = pl.ds(pl.multiple_of(row0 * W, W), count * W)
                DR[t, rows, :] = drive[at : at + count * W]
                at += count * W
        for row0, count in spans:
            rows = pl.ds(pl.multiple_of(row0 * W, W), count * W)
            for i in range(T):
                value = COEF[T + i : T + i + 1] * DR[frame_of(i), rows, :]
                if i:
                    value = value + COEF[i : i + 1] * LS[i - 1, rows, :]
                LS[i, rows, :] = value
            FIN[rows, :] = encode(last * value)
            send_finals(row0, count)

    def rows_of(ref, k):
        return ref.at[pl.ds(pl.multiple_of(k * W, W), W)]

    def send_finals(row0, count):
        for r in range(count):
            k = row0 + lax.rem(r + tm, count)

            @pl.when(k != tm)
            def _():
                remote(
                    rows_of(FIN, k), RF.at[tm], fin_send.at[k], carry_recv.at[1], (k, tile)
                ).start()

    took(X.at[:, pl.ds(1, R)], load_sem.at[0])
    widen(X, X3, 1 + core * R, R)
    local_scan((core * R + 1, R - 2))
    took(X.at[:, pl.ds(1, R)], in_recv.at[0])
    widen(X, X3, 1 + (1 - core) * R, R)
    if R > 2:
        local_scan(((1 - core) * (R - 1) + core, R))
    else:
        local_scan((1, RC - 2))
    edge_took(0, X)
    widen(X, X3, 0, 1)
    widen(X, X3, RC + 1, 1)
    local_scan((0, 1), (RC - 1, 1))

    others = pl.ds(0, nt - 1)
    RF[tm] = FIN[pl.ds(pl.multiple_of(tm * W, W), W), :]

    weights(WB, w_out, w_in)
    took(Y.at[:, pl.ds(1, R)], load_sem.at[1])
    took(Y.at[:, pl.ds(1, R)], in_recv.at[1])
    edge_took(1, Y)
    widen(Y, Y3, 0, RC + 2)

    took(DG.at[others], carry_recv.at[0])
    took(RF.at[others], carry_recv.at[1])
    carry = jnp.zeros((W, CH), F32)
    for i in range(nt):
        k = core * i + (1 - core) * (nt - 1 - i)
        EF[k] = encode(carry)

        @pl.when(k != tm)
        def _():
            remote(EF.at[k], rows_of(INC, tm), back_send.at[k], inc_recv.at[tm], (k, tile)).start()

        if i < nt - 1:
            carry = DG[k, 0:1, :] * carry + decode(RF[k])
    INC[pl.ds(pl.multiple_of(tm * W, W), W), :] = EF[tm]

    def finish(row0, count):
        for k in range(row0, row0 + count):

            @pl.when(tm != k)
            def _():
                took(rows_of(INC, k), inc_recv.at[k])

        rows = slice(row0 * W, (row0 + count) * W)
        incoming = decode(INC[rows, :])
        for i in range(T):
            value = (
                COEF[2 * T + i : 2 * T + i + 1] * LS[i, rows, :]
                + COEF[3 * T + i : 3 * T + i + 1] * incoming
            )
            S[frame_of(i), 1 + row0 : 1 + row0 + count] = value.astype(BF16).reshape(count, W, CH)

    finish(1, RC - 2)
    finish(0, 1)
    finish(RC - 1, 1)

    up = remote(
        S.at[:, pl.ds(1, 1)], S.at[:, pl.ds(RC + 1, 1)], halo_send.at[2, 0], halo_recv.at[2, 1],
        (tm, lax.max(y - 1, 0) * 2 + core),
    )
    down = remote(
        S.at[:, pl.ds(RC, 1)], S.at[:, pl.ds(0, 1)], halo_send.at[2, 1], halo_recv.at[2, 0],
        (tm, lax.min(y + 1, ny - 1) * 2 + core),
    )

    @pl.when(y > 0)
    def _():
        up.start()

    @pl.when(y < ny - 1)
    def _():
        down.start()

    orders = (("x", "y", "z"), ("y", "z", "x"), ("z", "x", "y"))
    steps = [(da, db) for da in range(n) for db in range(n) if da or db]
    steps.sort(key=lambda s: -sum(min(d, n - d) for d in s))

    def place(g, da, db):
        a, b = orders[g][:2]
        return lax.rem(where_on[a] + da, n) * n + lax.rem(where_on[b] + db, n)

    def plane_peer(g, da, db):
        at = dict(where_on)
        for axis, d in zip(orders[g], (da, db)):
            at[axis] = lax.rem(at[axis] + d, n)
        return (at["z"] * nx + at["x"], at["y"] * 2 + core)

    for t in range(T):
        ST[t] = S[t, 1 : RC + 1].reshape(pos, CH).T
    for g in range(3):
        first = core * (2 - g) + (1 - core) * g
        total = jnp.zeros((CH, 3 * CH), F32)
        for t in range(T):
            other = Y3[t, pl.ds(first, RC)].reshape(pos, 3 * CH)
            total = total + jnp.dot(ST[t], other, preferred_element_type=F32)
        total = total * factor

        @pl.when(forward)
        def _():
            for j in range(3):
                block = total[:, (2 - j) * CH : (3 - j) * CH]
                G[(g * 3 + j) * CH : (g * 3 + j + 1) * CH, :] = block
                GC[(g * 3 + j) * CH : (g * 3 + j + 1) * CH, :] = encode(block)

        @pl.when(core == 0)
        def _():
            for j in range(3):
                block = total[:, j * CH : (j + 1) * CH].T
                G[(g * 3 + j) * CH : (g * 3 + j + 1) * CH, :] = block
                GC[(g * 3 + j) * CH : (g * 3 + j + 1) * CH, :] = encode(block)

        for slot, (da, db) in enumerate(steps):
            q = place(g, da, db)
            remote(
                GC.at[pl.ds(pl.multiple_of(g * group + q * chunk, chunk), chunk)],
                R1.at[g, slot], ar_send.at[0], ar_recv.at[g], plane_peer(g, da, db),
            ).start()

    def conv_out(t):
        for side, (start, stage) in enumerate(((core * R, own_out), ((1 - core) * R, MO))):
            rows = pl.ds(start + 1, R)
            direct = skip[...] * X[t, rows].reshape(R * W, CH).astype(F32)
            value = conv(S3, t, start, R, WB) + direct
            stage[t] = value.astype(BF16).reshape(R, W, CH)
        remote(MO.at[t], mate_out.at[t], mo_send.at[t], mo_recv.at[t], mate).start()

    widen(S, S3, 1, RC)

    @pl.when(y > 0)
    def _():
        took(S.at[:, pl.ds(0, 1)], halo_recv.at[2, 0])

    @pl.when(y < ny - 1)
    def _():
        took(S.at[:, pl.ds(0, 1)], halo_recv.at[2, 1])

    widen(S, S3, 0, 1)
    widen(S, S3, RC + 1, 1)

    conv_out(0)
    conv_out(1)
    for g in range(3):
        took(R1.at[g], ar_recv.at[g])
        value = G[pl.ds(pl.multiple_of(g * group + place(g, 0, 0) * chunk, chunk), chunk), :]
        for slot in range(n * n - 1):
            value = value + decode(R1[g, slot])
        c = orders[g][2]
        r = where_on[c]
        R3[g, r] = value
        for d in range(1, n):
            remote(
                R3.at[g, r], R3.at[g, r], ar_send.at[1], ar_recv.at[3 + g], axis_peer(c, d)
            ).start()
    conv_out(2)
    base = core * half
    for g in range(3):
        took(R3.at[g, pl.ds(0, n - 1)], ar_recv.at[3 + g])
        value = R3[g, 0]
        for k in range(1, n):
            value = value + R3[g, k]
        rows = pl.ds(pl.multiple_of(base + g * group + place(g, 0, 0) * chunk, chunk), chunk)
        sums[rows, :] = value.astype(BF16)
        for da, db in steps:
            peer = plane_peer(g, da, db)
            remote(
                sums.at[rows], sums.at[rows], ar_send.at[2], ar_recv.at[6 + g], peer
            ).start()
            other = (peer[0], peer[1] + 1 - 2 * core)
            remote(
                sums.at[rows], sums.at[rows], ar_send.at[3], ar_recv.at[9 + g], other
            ).start()
        remote(sums.at[rows], sums.at[rows], ar_send.at[4], ar_recv.at[9 + g], mate).start()
    conv_out(3)
    for g in range(3):
        took(sums.at[pl.ds(0, group - chunk)], ar_recv.at[6 + g])
        took(sums.at[pl.ds(0, group)], ar_recv.at[9 + g])

    for t in range(T):
        took(MO.at[t], mo_recv.at[t])

    for t in range(T):
        took(MO.at[t], mo_send.at[t])
    took(R1, ar_send.at[0])
    took(R3.at[:, pl.ds(0, n - 1)], ar_send.at[1])
    took(sums.at[pl.ds(0, half - 3 * chunk)], ar_send.at[2])
    took(sums.at[pl.ds(0, half - 3 * chunk)], ar_send.at[3])
    took(sums.at[pl.ds(0, 3 * chunk)], ar_send.at[4])
    took(DG.at[others], carry_send.at[0])
    for k in range(nt):

        @pl.when(tm != k)
        def _():
            took(EF.at[0], fin_send.at[k])
            took(EF.at[0], back_send.at[k])

    for k in range(2):
        took(X.at[:, pl.ds(1, R)], in_send.at[k])

    @pl.when(has_next)
    def _():
        for which in range(2):
            for copy in edge_copies(which):
                copy.wait_send()

    @pl.when(y > 0)
    def _():
        up.wait_send()

    @pl.when(y < ny - 1)
    def _():
        down.wait_send()


def store_kernel(own_out, mate_out, sums, output, grad_frames, grad_in, grad_out, wide, sem):
    forward = lax.rem(lax.axis_index("tile"), 2) == 1
    half = grad_in.shape[0]

    def put(first, second):
        pltpu.make_async_copy(own_out, first, sem.at[0]).start()
        pltpu.make_async_copy(mate_out, second, sem.at[1]).start()

    @pl.when(forward)
    def _():
        put(output, grad_frames)

    @pl.when(jnp.logical_not(forward))
    def _():
        put(grad_frames, output)

    copies = []
    for k, dst in enumerate((grad_in, grad_out)):
        wide[k] = sums[k * half : (k + 1) * half, :].astype(F32)
        copies.append(pltpu.make_async_copy(wide.at[k], dst, sem.at[2 + k]))
        copies[-1].start()
    pltpu.make_async_copy(own_out, output, sem.at[0]).wait()
    pltpu.make_async_copy(mate_out, grad_frames, sem.at[1]).wait()
    for copy in copies:
        copy.wait()


def solution(mesh):
    nt, ntile = mesh.shape["tm"], mesh.shape["tile"]
    nx = math.isqrt(nt)
    ny = ntile // 2

    def step(frames, cot, w_in, w_out, skip, log_decay):
        T, R, W, CH = frames.shape
        factor = 1.0 / math.sqrt(T * nt * R * ntile * W)
        RC = 2 * R
        pos = RC * W
        n = nx
        half = 9 * CH
        chunk = half // 3 // (n * n)
        vm = pltpu.VMEM
        field = vm((T, RC + 2, W, CH), BF16)
        field3 = vm((T, RC + 2, W, 3 * CH), BF16)
        dma = pltpu.SemaphoreType.DMA
        hbm = pl.BlockSpec(memory_space=pl.ANY)
        vmem = pl.BlockSpec(memory_space=pltpu.VMEM)
        own_out, mate_out, sums = pl.pallas_call(
            functools.partial(chain_kernel, (nt, nx, ny, factor)),
            out_shape=(
                vm(frames.shape, BF16),
                vm(frames.shape, BF16),
                vm((2 * half, CH), BF16),
            ),
            in_specs=[hbm] * 6,
            out_specs=[vmem] * 3,
            scratch_shapes=[
                field, field, field, field3, field3, field3, vm((T, CH, pos), BF16),
                vm((half, CH), BF16), vm((half, CH), BF16), vm((1, CH), F32), vm((T, CH), F32),
                vm((half, CH), BF16), vm((half, CH), BF16), vm((4 * T, CH), F32), vm((nt, 8, CH), F32),
                vm((T, pos, CH), F32), vm((T, pos, CH), F32), vm((pos, CH), BF16),
                vm((nt, W, CH), BF16), vm((nt, W, CH), BF16), vm((pos, CH), BF16),
                vm((half, CH), F32), vm((half, CH), BF16),
                vm((3, n * n - 1, chunk, CH), BF16), vm((3, n, chunk, CH), F32), vm(frames.shape, BF16),
                dma((6,)), dma((2,)), dma((2,)), dma((3, 2)), dma((3, 2)),
                dma((1,)), dma((2,)), dma((nt,)), dma((nt,)), dma((nt,)),
                dma((6,)), dma((12,)), dma((T,)), dma((T,)),
            ],
            compiler_params=pltpu.CompilerParams(
                collective_id=0, has_side_effects=True, vmem_limit_bytes=65_300_000
            ),
        )(
            frames, cot, w_in.reshape(half, CH), w_out.reshape(half, CH),
            skip.reshape(1, CH), log_decay,
        )
        res = pl.pallas_call(
            store_kernel,
            out_shape=(
                jax.ShapeDtypeStruct(frames.shape, BF16),
                jax.ShapeDtypeStruct(frames.shape, BF16),
                jax.ShapeDtypeStruct((half, CH), F32),
                jax.ShapeDtypeStruct((half, CH), F32),
            ),
            in_specs=[vmem] * 3,
            out_specs=[hbm] * 4,
            scratch_shapes=[vm((2, half, CH), F32), dma((4,))],
            compiler_params=pltpu.CompilerParams(vmem_limit_bytes=8 * 2**20),
        )(own_out, mate_out, sums)
        return (res[0], res[1], res[2].reshape(3, 3, CH, CH), res[3].reshape(3, 3, CH, CH))

    block = P("tm", "tile", None, None)
    return jax.shard_map(
        step,
        mesh=mesh,
        in_specs=(block, block, P(), P(), P(), P("tm", None)),
        out_specs=(block, block, P(), P()),
        check_vma=False,
    )
```

```python
import functools
import math

import jax
import jax.numpy as jnp
from jax import lax
from jax.experimental import pallas as pl
from jax.experimental.pallas import tpu as pltpu
from jax.sharding import PartitionSpec as P

MESH = pl.DeviceIdType.MESH
F32 = jnp.float32
BF16 = jnp.bfloat16
ROOT = 5


def encode(v):
    square = v * v
    return (v * (square * square)).astype(BF16)


def decode(code):
    w = code.astype(F32)
    root = jnp.exp2(jnp.log2(jnp.abs(w)) * (1.0 / ROOT))
    return jnp.where(w < 0.0, -root, root)


def chain_kernel(
    dims,
    frames, cot, w_in_hbm, w_out_hbm, skip_hbm, log_decay_hbm,
    own_out, mate_out, sums,
    X, Y, S, X3, Y3, S3, ST,
    w_in, w_out, skip, log_decay, WA, WB, COEF, DG,
    DR, LS, FIN, RF, EF, INC,
    G, GC, R1, R3, MO,
    load_sem, in_send, in_recv, halo_send, halo_recv,
    carry_send, carry_recv, fin_send, back_send, inc_recv, ar_send, ar_recv, mo_send, mo_recv,
):
    nt, nx, ny, factor = dims
    T, R, W, CH = frames.shape
    RC = 2 * R
    n = nx
    pos = RC * W
    half = 9 * CH
    group = half // 3
    chunk = group // (n * n)

    tm = lax.axis_index("tm")
    tile = lax.axis_index("tile")
    ntile = ny * 2
    z, x = lax.div(tm, nx), lax.rem(tm, nx)
    y, core = lax.div(tile, 2), lax.rem(tile, 2)
    forward = core == 1
    mate = (tm, y * 2 + 1 - core)

    def on_tm(d):
        return (lax.rem(tm + d, nt), tile)

    where_on = {"x": x, "y": y, "z": z}

    def axis_peer(axis, d):
        if axis == "x":
            return (z * nx + lax.rem(x + d, nx), tile)
        if axis == "z":
            return (lax.rem(z + d, nt // nx) * nx + x, tile)
        return (tm, lax.rem(y + d, ny) * 2 + core)

    def remote(src, dst, send, recv, device):
        return pltpu.make_async_remote_copy(
            src, dst, send, recv, device_id=device, device_id_type=MESH
        )

    def took(ref, sem):
        pltpu.make_async_copy(ref, ref, sem).wait()

    barrier = pltpu.get_barrier_semaphore()
    for d in range(1, nt):
        pl.semaphore_signal(barrier, inc=1, device_id=on_tm(d), device_id_type=MESH)
    for d in range(1, ntile):
        pl.semaphore_signal(
            barrier, inc=1, device_id=(tm, lax.rem(tile + d, ntile)), device_id_type=MESH
        )

    own_rows = pl.ds(1 + core * R, R)
    small = [
        pltpu.make_async_copy(src, dst, load_sem.at[2 + k])
        for k, (src, dst) in enumerate(
            (
                (log_decay_hbm, log_decay), (w_in_hbm, w_in), (w_out_hbm, w_out), (skip_hbm, skip),
            )
        )
    ]

    def load(first, second):
        pltpu.make_async_copy(first, X.at[:, own_rows], load_sem.at[0]).start()
        pltpu.make_async_copy(second, Y.at[:, own_rows], load_sem.at[1]).start()

    @pl.when(forward)
    def _():
        load(frames, cot)

    @pl.when(core == 0)
    def _():
        load(cot, frames)

    for copy in small:
        copy.start()

    pl.semaphore_wait(barrier, nt - 1 + ntile - 1)

    def send_inputs(first, second):
        remote(first, X.at[:, own_rows], in_send.at[0], in_recv.at[0], mate).start()
        edge(0)
        remote(second, Y.at[:, own_rows], in_send.at[1], in_recv.at[1], mate).start()
        edge(1)

    edge_src = pl.ds(core * (R - 1), 1)
    edge_dst = pl.ds((1 - core) * (RC + 1), 1)
    next_y = y + 2 * core - 1
    has_next = (next_y >= 0) & (next_y < ny)
    safe_y = lax.min(lax.max(next_y, 0), ny - 1)

    def edge_copies(which):
        copies = []
        for c in range(2):
            src = (frames, cot)[(c == 1) == (which == 1)]
            dst = (X, Y)[which]
            copies.append(
                remote(
                    src.at[:, edge_src], dst.at[:, edge_dst],
                    halo_send.at[which, c], halo_recv.at[which, 1 - core],
                    (tm, safe_y * 2 + c),
                )
            )
        return copies

    def edge(which):
        @pl.when(has_next)
        def _():
            for copy in edge_copies(which):
                copy.start()

    @pl.when(forward)
    def _():
        send_inputs(cot, frames)

    @pl.when(core == 0)
    def _():
        send_inputs(frames, cot)

    def edge_took(which, field):
        @pl.when(y > 0)
        def _():
            took(field.at[:, pl.ds(0, 1)], halo_recv.at[which, 0])

        @pl.when(y < ny - 1)
        def _():
            took(field.at[:, pl.ds(RC + 1, 1)], halo_recv.at[which, 1])

    small[0].wait()
    dec = jnp.exp(log_decay[...])
    whole = dec[0:1]
    for t in range(1, T):
        whole = whole * dec[t : t + 1]
    DG[tm] = jnp.broadcast_to(whole, (8, CH))
    one = jnp.ones((1, CH), F32)
    reach = None
    for i in range(T):
        a = jnp.where(forward, dec[i : i + 1], one if i == 0 else dec[T - i : T - i + 1])
        b = jnp.where(forward, 1.0 - dec[i : i + 1], one)
        c = jnp.where(forward, one, 1.0 - dec[T - 1 - i : T - i])
        reach = a if reach is None else reach * a
        COEF[i : i + 1] = a
        COEF[T + i : T + i + 1] = b
        COEF[2 * T + i : 2 * T + i + 1] = c
        COEF[3 * T + i : 3 * T + i + 1] = c * reach
    last = jnp.where(forward, one, dec[0:1])

    def weights(dst, plain, turned):
        @pl.when(forward)
        def _():
            dst[...] = plain[...]

        @pl.when(core == 0)
        def _():
            for k in range(9):
                dst[k * CH : (k + 1) * CH, :] = turned[(8 - k) * CH : (9 - k) * CH, :].T

    for copy in small[1:]:
        copy.wait()
    weights(WA, w_in, w_out)

    for d in range(1, nt):
        remote(DG.at[tm], DG.at[tm], carry_send.at[0], carry_recv.at[0], on_tm(d)).start()

    @pl.when(y == 0)
    def _():
        for field in (X, Y, S):
            field[:, 0] = jnp.zeros((T, W, CH), BF16)

    @pl.when(y == ny - 1)
    def _():
        for field in (X, Y, S):
            field[:, RC + 1] = jnp.zeros((T, W, CH), BF16)

    col = lax.broadcasted_iota(jnp.int32, (1, W, CH), 1)

    def widen(src, dst, row0, count):
        def step(k, _):
            r = row0 + k
            for t in range(T):
                v = src[t, pl.ds(r, 1)].astype(F32)
                left = jnp.where(col == 0, 0.0, pltpu.roll(v, 1, 1))
                right = jnp.where(col == W - 1, 0.0, pltpu.roll(v, W - 1, 1))
                dst[t, pl.ds(r, 1), :, 0:CH] = left.astype(BF16)
                dst[t, pl.ds(r, 1), :, CH : 2 * CH] = src[t, pl.ds(r, 1)]
                dst[t, pl.ds(r, 1), :, 2 * CH : 3 * CH] = right.astype(BF16)
            return 0

        lax.fori_loop(0, count, step, 0)

    def conv(src3, t, row0, count, weight):
        taps = jnp.concatenate(
            [src3[t, pl.ds(row0 + i, count)].reshape(count * W, 3 * CH) for i in range(3)], axis=-1
        )
        return jnp.dot(taps, weight[...], preferred_element_type=F32)

    def frame_of(i):
        return core * i + (1 - core) * (T - 1 - i)

    def local_scan(*spans):
        spans = [span for span in spans if span[1]]
        if not spans:
            return
        taps = jnp.concatenate(
            [
                jnp.concatenate([X3[:, pl.ds(row0 + i, count)] for row0, count in spans], axis=1)
                .reshape(-1, 3 * CH)
                for i in range(3)
            ],
            axis=-1,
        )
        drive = jnp.dot(taps, WA[...], preferred_element_type=F32)
        per_frame = drive.shape[0] // T
        for t in range(T):
            at = t * per_frame
            for row0, count in spans:
                rows = pl.ds(pl.multiple_of(row0 * W, W), count * W)
                DR[t, rows, :] = drive[at : at + count * W]
                at += count * W
        for row0, count in spans:
            rows = pl.ds(pl.multiple_of(row0 * W, W), count * W)
            for i in range(T):
                value = COEF[T + i : T + i + 1] * DR[frame_of(i), rows, :]
                if i:
                    value = value + COEF[i : i + 1] * LS[i - 1, rows, :]
                LS[i, rows, :] = value
            FIN[rows, :] = encode(last * value)
            send_finals(row0, count)

    def rows_of(ref, k):
        return ref.at[pl.ds(pl.multiple_of(k * W, W), W)]

    farthest_first = [
        lax.rem(z + dz, n) * n + lax.rem(x + dx, n)
        for dz, dx in sorted(
            ((dz, dx) for dz in range(n) for dx in range(n) if dz or dx),
            key=lambda s: -sum(min(d, n - d) for d in s),
        )
    ]

    def send_finals(row0, count):
        for k in farthest_first:

            @pl.when((k >= row0) & (k < row0 + count))
            def _():
                remote(
                    rows_of(FIN, k), RF.at[tm], fin_send.at[k], carry_recv.at[1], (k, tile)
                ).start()

    took(X.at[:, pl.ds(1, R)], load_sem.at[0])
    widen(X, X3, 1 + core * R, R)
    local_scan((core * R + 1, R - 2))
    took(X.at[:, pl.ds(1, R)], in_recv.at[0])
    widen(X, X3, 1 + (1 - core) * R, R)
    if R > 2:
        local_scan(((1 - core) * (R - 1) + core, R))
    else:
        local_scan((1, RC - 2))
    edge_took(0, X)
    widen(X, X3, 0, 1)
    widen(X, X3, RC + 1, 1)
    local_scan((0, 1), (RC - 1, 1))

    others = pl.ds(0, nt - 1)
    RF[tm] = FIN[pl.ds(pl.multiple_of(tm * W, W), W), :]

    weights(WB, w_out, w_in)
    took(Y.at[:, pl.ds(1, R)], load_sem.at[1])
    took(Y.at[:, pl.ds(1, R)], in_recv.at[1])
    edge_took(1, Y)
    widen(Y, Y3, 0, RC + 2)

    took(DG.at[others], carry_recv.at[0])
    took(RF.at[others], carry_recv.at[1])
    carry = jnp.zeros((W, CH), F32)
    for i in range(nt):
        k = core * i + (1 - core) * (nt - 1 - i)
        EF[k] = encode(carry)

        if i < nt - 1:
            carry = DG[k, 0:1, :] * carry + decode(RF[k])
    for k in farthest_first:
        remote(EF.at[k], rows_of(INC, tm), back_send.at[k], inc_recv.at[tm], (k, tile)).start()
    INC[pl.ds(pl.multiple_of(tm * W, W), W), :] = EF[tm]

    def finish(row0, count):
        for k in range(row0, row0 + count):

            @pl.when(tm != k)
            def _():
                took(rows_of(INC, k), inc_recv.at[k])

        rows = slice(row0 * W, (row0 + count) * W)
        incoming = decode(INC[rows, :])
        for i in range(T):
            value = (
                COEF[2 * T + i : 2 * T + i + 1] * LS[i, rows, :]
                + COEF[3 * T + i : 3 * T + i + 1] * incoming
            )
            S[frame_of(i), 1 + row0 : 1 + row0 + count] = value.astype(BF16).reshape(count, W, CH)

    finish(1, RC - 2)
    finish(0, 1)
    finish(RC - 1, 1)

    up = remote(
        S.at[:, pl.ds(1, 1)], S.at[:, pl.ds(RC + 1, 1)], halo_send.at[2, 0], halo_recv.at[2, 1],
        (tm, lax.max(y - 1, 0) * 2 + core),
    )
    down = remote(
        S.at[:, pl.ds(RC, 1)], S.at[:, pl.ds(0, 1)], halo_send.at[2, 1], halo_recv.at[2, 0],
        (tm, lax.min(y + 1, ny - 1) * 2 + core),
    )

    @pl.when(y > 0)
    def _():
        up.start()

    @pl.when(y < ny - 1)
    def _():
        down.start()

    orders = (("x", "y", "z"), ("y", "z", "x"), ("z", "x", "y"))
    steps = [(da, db) for da in range(n) for db in range(n) if da or db]
    steps.sort(key=lambda s: -sum(min(d, n - d) for d in s))

    def place(g, da, db):
        a, b = orders[g][:2]
        return lax.rem(where_on[a] + da, n) * n + lax.rem(where_on[b] + db, n)

    def plane_peer(g, da, db):
        at = dict(where_on)
        for axis, d in zip(orders[g], (da, db)):
            at[axis] = lax.rem(at[axis] + d, n)
        return (at["z"] * nx + at["x"], at["y"] * 2 + core)

    for t in range(T):
        ST[t] = S[t, 1 : RC + 1].reshape(pos, CH).T
    for g in range(3):
        first = core * (2 - g) + (1 - core) * g
        total = jnp.zeros((CH, 3 * CH), F32)
        for t in range(T):
            other = Y3[t, pl.ds(first, RC)].reshape(pos, 3 * CH)
            total = total + jnp.dot(ST[t], other, preferred_element_type=F32)
        total = total * factor

        @pl.when(forward)
        def _():
            for j in range(3):
                block = total[:, (2 - j) * CH : (3 - j) * CH]
                G[(g * 3 + j) * CH : (g * 3 + j + 1) * CH, :] = block
                GC[(g * 3 + j) * CH : (g * 3 + j + 1) * CH, :] = encode(block)

        @pl.when(core == 0)
        def _():
            for j in range(3):
                block = total[:, j * CH : (j + 1) * CH].T
                G[(g * 3 + j) * CH : (g * 3 + j + 1) * CH, :] = block
                GC[(g * 3 + j) * CH : (g * 3 + j + 1) * CH, :] = encode(block)

        for slot, (da, db) in enumerate(steps):
            q = place(g, da, db)
            remote(
                GC.at[pl.ds(pl.multiple_of(g * group + q * chunk, chunk), chunk)],
                R1.at[g, slot], ar_send.at[0], ar_recv.at[g], plane_peer(g, da, db),
            ).start()

    def conv_out(t):
        for side, (start, stage) in enumerate(((core * R, own_out), ((1 - core) * R, MO))):
            rows = pl.ds(start + 1, R)
            direct = skip[...] * X[t, rows].reshape(R * W, CH).astype(F32)
            value = conv(S3, t, start, R, WB) + direct
            stage[t] = value.astype(BF16).reshape(R, W, CH)
        remote(MO.at[t], mate_out.at[t], mo_send.at[t], mo_recv.at[t], mate).start()

    widen(S, S3, 1, RC)

    @pl.when(y > 0)
    def _():
        took(S.at[:, pl.ds(0, 1)], halo_recv.at[2, 0])

    @pl.when(y < ny - 1)
    def _():
        took(S.at[:, pl.ds(0, 1)], halo_recv.at[2, 1])

    widen(S, S3, 0, 1)
    widen(S, S3, RC + 1, 1)

    conv_out(0)
    conv_out(1)
    for g in range(3):
        took(R1.at[g], ar_recv.at[g])
        value = G[pl.ds(pl.multiple_of(g * group + place(g, 0, 0) * chunk, chunk), chunk), :]
        for slot in range(n * n - 1):
            value = value + decode(R1[g, slot])
        c = orders[g][2]
        r = where_on[c]
        R3[g, r] = value
        for d in range(1, n):
            remote(
                R3.at[g, r], R3.at[g, r], ar_send.at[1], ar_recv.at[3 + g], axis_peer(c, d)
            ).start()
    conv_out(2)
    base = core * half
    for g in range(3):
        took(R3.at[g, pl.ds(0, n - 1)], ar_recv.at[3 + g])
        value = R3[g, 0]
        for k in range(1, n):
            value = value + R3[g, k]
        rows = pl.ds(pl.multiple_of(base + g * group + place(g, 0, 0) * chunk, chunk), chunk)
        sums[rows, :] = value.astype(BF16)
        for da, db in steps:
            peer = plane_peer(g, da, db)
            remote(
                sums.at[rows], sums.at[rows], ar_send.at[2], ar_recv.at[6 + g], peer
            ).start()
            other = (peer[0], peer[1] + 1 - 2 * core)
            remote(
                sums.at[rows], sums.at[rows], ar_send.at[3], ar_recv.at[9 + g], other
            ).start()
        remote(sums.at[rows], sums.at[rows], ar_send.at[4], ar_recv.at[9 + g], mate).start()
    conv_out(3)
    for g in range(3):
        took(sums.at[pl.ds(0, group - chunk)], ar_recv.at[6 + g])
        took(sums.at[pl.ds(0, group)], ar_recv.at[9 + g])

    for t in range(T):
        took(MO.at[t], mo_recv.at[t])

    for t in range(T):
        took(MO.at[t], mo_send.at[t])
    took(R1, ar_send.at[0])
    took(R3.at[:, pl.ds(0, n - 1)], ar_send.at[1])
    took(sums.at[pl.ds(0, half - 3 * chunk)], ar_send.at[2])
    took(sums.at[pl.ds(0, half - 3 * chunk)], ar_send.at[3])
    took(sums.at[pl.ds(0, 3 * chunk)], ar_send.at[4])
    took(DG.at[others], carry_send.at[0])
    for k in range(nt):

        @pl.when(tm != k)
        def _():
            took(EF.at[0], fin_send.at[k])
            took(EF.at[0], back_send.at[k])

    for k in range(2):
        took(X.at[:, pl.ds(1, R)], in_send.at[k])

    @pl.when(has_next)
    def _():
        for which in range(2):
            for copy in edge_copies(which):
                copy.wait_send()

    @pl.when(y > 0)
    def _():
        up.wait_send()

    @pl.when(y < ny - 1)
    def _():
        down.wait_send()


def store_kernel(own_out, mate_out, sums, output, grad_frames, grad_in, grad_out, wide, sem):
    forward = lax.rem(lax.axis_index("tile"), 2) == 1
    half = grad_in.shape[0]

    def put(first, second):
        pltpu.make_async_copy(own_out, first, sem.at[0]).start()
        pltpu.make_async_copy(mate_out, second, sem.at[1]).start()

    @pl.when(forward)
    def _():
        put(output, grad_frames)

    @pl.when(jnp.logical_not(forward))
    def _():
        put(grad_frames, output)

    copies = []
    for k, dst in enumerate((grad_in, grad_out)):
        wide[k] = sums[k * half : (k + 1) * half, :].astype(F32)
        copies.append(pltpu.make_async_copy(wide.at[k], dst, sem.at[2 + k]))
        copies[-1].start()
    pltpu.make_async_copy(own_out, output, sem.at[0]).wait()
    pltpu.make_async_copy(mate_out, grad_frames, sem.at[1]).wait()
    for copy in copies:
        copy.wait()


def solution(mesh):
    nt, ntile = mesh.shape["tm"], mesh.shape["tile"]
    nx = math.isqrt(nt)
    ny = ntile // 2

    def step(frames, cot, w_in, w_out, skip, log_decay):
        T, R, W, CH = frames.shape
        factor = 1.0 / math.sqrt(T * nt * R * ntile * W)
        RC = 2 * R
        pos = RC * W
        n = nx
        half = 9 * CH
        chunk = half // 3 // (n * n)
        vm = pltpu.VMEM
        field = vm((T, RC + 2, W, CH), BF16)
        field3 = vm((T, RC + 2, W, 3 * CH), BF16)
        dma = pltpu.SemaphoreType.DMA
        hbm = pl.BlockSpec(memory_space=pl.ANY)
        vmem = pl.BlockSpec(memory_space=pltpu.VMEM)
        own_out, mate_out, sums = pl.pallas_call(
            functools.partial(chain_kernel, (nt, nx, ny, factor)),
            out_shape=(
                vm(frames.shape, BF16),
                vm(frames.shape, BF16),
                vm((2 * half, CH), BF16),
            ),
            in_specs=[hbm] * 6,
            out_specs=[vmem] * 3,
            scratch_shapes=[
                field, field, field, field3, field3, field3, vm((T, CH, pos), BF16),
                vm((half, CH), BF16), vm((half, CH), BF16), vm((1, CH), F32), vm((T, CH), F32),
                vm((half, CH), BF16), vm((half, CH), BF16), vm((4 * T, CH), F32), vm((nt, 8, CH), F32),
                vm((T, pos, CH), F32), vm((T, pos, CH), F32), vm((pos, CH), BF16),
                vm((nt, W, CH), BF16), vm((nt, W, CH), BF16), vm((pos, CH), BF16),
                vm((half, CH), F32), vm((half, CH), BF16),
                vm((3, n * n - 1, chunk, CH), BF16), vm((3, n, chunk, CH), F32), vm(frames.shape, BF16),
                dma((6,)), dma((2,)), dma((2,)), dma((3, 2)), dma((3, 2)),
                dma((1,)), dma((2,)), dma((nt,)), dma((nt,)), dma((nt,)),
                dma((6,)), dma((12,)), dma((T,)), dma((T,)),
            ],
            compiler_params=pltpu.CompilerParams(
                collective_id=0, has_side_effects=True, vmem_limit_bytes=65_300_000
            ),
        )(
            frames, cot, w_in.reshape(half, CH), w_out.reshape(half, CH),
            skip.reshape(1, CH), log_decay,
        )
        res = pl.pallas_call(
            store_kernel,
            out_shape=(
                jax.ShapeDtypeStruct(frames.shape, BF16),
                jax.ShapeDtypeStruct(frames.shape, BF16),
                jax.ShapeDtypeStruct((half, CH), F32),
                jax.ShapeDtypeStruct((half, CH), F32),
            ),
            in_specs=[vmem] * 3,
            out_specs=[hbm] * 4,
            scratch_shapes=[vm((2, half, CH), F32), dma((4,))],
            compiler_params=pltpu.CompilerParams(vmem_limit_bytes=8 * 2**20),
        )(own_out, mate_out, sums)
        return (res[0], res[1], res[2].reshape(3, 3, CH, CH), res[3].reshape(3, 3, CH, CH))

    block = P("tm", "tile", None, None)
    return jax.shard_map(
        step,
        mesh=mesh,
        in_specs=(block, block, P(), P(), P(), P("tm", None)),
        out_specs=(block, block, P(), P()),
        check_vma=False,
    )
```
